32 devices in a mesh: var: 4 (over x, core), dp: 8 (over z, y).
Axes of the slice: x: 2, y: 2, z: 4, core: 2. Of those that a mesh axis runs over, the one named last changes fastest.
Arguments:
- pixels: bfloat16 [72, 4, 8, 1024], P('var', None, 'dp'), may hold values from -6 to 6
- var_mask: int32 [72], P('var'), may hold values from 0 to 1, as said below
- lengths: int32 [8], P('dp'), may hold values from 64 to 1024, as said below
- condition: bfloat16 [8, 384], P('dp'), may hold values from -6 to 6
- cotangent: float32 [8, 1024, 384], P('dp', 'var'), may hold values from -6 to 6
- master: float32 [5898240], P(('var', 'dp'))
- moment_one: float32 [5898240], P(('var', 'dp')), may hold values from -6 to 6
- moment_two: float32 [5898240], P(('var', 'dp')), may hold values from 0.1024 to 1.6384
Outputs:
- output: float32 [8, 1024, 384], P('dp', 'var')
- pixel_grad: float32 [72, 4, 8, 1024], P('var', None, 'dp')
- grad_norm: float32 [], replicated
- new_master: float32 [5898240], P(('var', 'dp'))
- new_moment_one: float32 [5898240], P(('var', 'dp'))
- new_moment_two: float32 [5898240], P(('var', 'dp'))
- new_copy: bfloat16 [5898240], P(('var', 'dp'))
The draws below stay inside these ranges and needn't reach their ends.
Inputs may be any that keep to these rules, and one draw needn't show every extreme that they name: `lengths`: each sequence is a fine item of 1024 valid patches or a coarse item of 64 valid patches followed by padding. `var_mask`: variable 0 is always present.
All inputs are finite; a program needn't handle non-finite values.
Results may differ from the reference program's by a relative error of at most 0.022.
The reference program's roundings to bfloat16 on the way count: a program that leaves them out, or rounds other values in their place, can miss the bound.
Values may be sent and summed in bfloat16 or wider, within the bound.
No kernel may reach another device: no remote copies, remote signals or barrier semaphores. Data moves between devices by JAX's collectives and lax.ppermute only.
A program may use at most 256 MiB of HBM per device.

```python
import math
import jax
import jax.numpy as jnp
from jax import lax

D = 384
HEADS = 6
FF = 1536
VARS = 72
PIX = 4
LAYERS = 2
STEP = 3
SEQ = 1024
COARSE = 64
GROUPS = 8
TOKENS = 8192
PARAMS = 5866368
PADDED = 5898240


def draw_master(key, part):
    segments = [(VARS * PIX * D, 0.5), (D, 1.0), (2 * D * D, D ** (-0.5)), (D * D, D ** (-0.5))]
    for layer_idx in range(LAYERS):
        segments = segments + [(6 * D * D, D ** (-0.5)), (6 * D, 0.3), (3 * D * D, D ** (-0.5)), (D * D, 3.0 * D ** (-0.5)), (D * FF, D ** (-0.5)), (FF * D, 1.5 * FF ** (-0.5))]
    segments = segments + [(PADDED - PARAMS, 0.02)]
    scales = jnp.concatenate([jnp.full((entries,), spread, jnp.float32) for entries, spread in segments])
    return jax.random.normal(key, (PADDED,), jnp.float32) * scales


def draw_lengths(key, part):
    coins = jax.random.randint(key, (GROUPS,), 0, 2)
    order = jnp.arange(GROUPS)
    coins = jnp.where(order == 0, 1, jnp.where(order == 1, 0, coins))
    return jnp.where(coins == 1, SEQ, COARSE).astype(jnp.int32)


def draw_var_mask(key, part):
    picks = jax.random.randint(key, (VARS,), 0, 12)
    order = jnp.arange(VARS)
    present = jnp.where(picks == 0, 0, 1)
    present = jnp.where(order == 0, 1, jnp.where(order == VARS - 1, 0, present))
    return present.astype(jnp.int32)


def level_of(key, shape, cuts, least, largest):
    level = 1.0
    for position, shards_of in cuts:
        heights = jax.random.uniform(jax.random.fold_in(jax.random.fold_in(key, 6), position), (shards_of,), jnp.float32, least / len(cuts), largest / len(cuts))
        level = level * jnp.repeat(jnp.exp(heights), shape[position] // shards_of).reshape((-1,) + (1,) * (len(shape) - 1 - position))
    return level


def noise(rng, shape, scale, reach, cuts=(), held_as=jnp.bfloat16):
    array = jax.random.normal(rng, shape, jnp.float32) * scale
    if len(cuts) > 0:
        array = level_of(rng, shape, cuts, -0.22, 0.18) * array
    return jnp.clip(array, min=-reach, max=reach).astype(held_as)


def setup_inputs(seed: int = 0) -> dict:
    key_list = jax.random.split(jax.random.key(seed), 9)
    pixels = noise(key_list[0], (VARS, PIX, GROUPS, SEQ), 1.0, 6.0, ((0, 4), (2, 8)))
    var_mask = draw_var_mask(jax.random.fold_in(key_list[8], 71), 0)
    lengths = draw_lengths(jax.random.fold_in(key_list[8], 71), 0)
    condition = noise(key_list[3], (GROUPS, D), 1.0, 6.0, ((0, 8),))
    cotangent = noise(key_list[4], (GROUPS, SEQ, D), 1.0, 6.0, ((0, 8), (1, 4)), jnp.float32)
    master = draw_master(jax.random.fold_in(key_list[8], 71), 0)
    moment_one = noise(key_list[6], (PADDED,), (0.005 * TOKENS ** 0.5), 6.0, ((0, 32),), jnp.float32)
    moment_two = jnp.clip(0.1024 + 1.536 * jax.random.uniform(key_list[7], (PADDED,), jnp.float32) ** level_of(key_list[7], (PADDED,), ((0, 32),), -0.2, 0.2), 0.1024, 1.6384)
    return dict(pixels=pixels, var_mask=var_mask, lengths=lengths, condition=condition, cotangent=cotangent, master=master, moment_one=moment_one, moment_two=moment_two)


HIGH = lax.Precision.HIGHEST
NEG_BIG = -1e+30
NORM_EPS = 1e-06
CLIP_COEF = 0.005
LEARN_RATE = 0.06
WEIGHT_DECAY = 0.1
ADAM_EPS = 1e-08
BETA_ONE = 0.5
BETA_TWO = 0.5

@jax.custom_vjp
def low(v):
    return lax.optimization_barrier(v.astype(jnp.bfloat16)).astype(jnp.float32)

@jax.custom_vjp
def low_back(v):
    return v

def low_keep(v):
    return (low(v), None)

def low_pass(kept, grad):
    return (grad,)

def back_keep(v):
    return (v, None)

def back_low(kept, grad):
    return (low(grad),)
low.defvjp(low_keep, low_pass)
low_back.defvjp(back_keep, back_low)

def shape_list():
    shapes = [(VARS, PIX, D), (D,), (D, 2 * D), (D, D)]
    for layer_idx in range(LAYERS):
        shapes = shapes + [(D, 6 * D), (6 * D,), (D, 3 * D), (D, D), (D, FF), (FF, D)]
    return shapes

def unpack(flat_vec):
    segments = []
    offset = 0
    for extents in shape_list():
        entries = 1
        for extent in extents:
            entries = entries * extent
        segments.append(flat_vec[offset:offset + entries].reshape(extents))
        offset = offset + entries
    return segments

def pack(segments):
    flat_vec = jnp.concatenate([segment.reshape(-1) for segment in segments])
    return jnp.concatenate([flat_vec, jnp.zeros((PADDED - flat_vec.shape[0],), jnp.float32)])

def layer_norm(values):
    centered = values - lax.optimization_barrier(jnp.mean(values, axis=-1, keepdims=True))
    return centered * lax.rsqrt(lax.optimization_barrier(jnp.mean(centered * centered, axis=-1, keepdims=True)) + NORM_EPS)

def forward_group(weights, patches, var_mask, length, cond_vec):
    head_dim = D // HEADS
    score_scale = head_dim ** (-0.5)
    embed_weight, agg_query, kv_weight, agg_weight = weights[:4]

    def embed_one(inputs):
        patch_v, weight_v = inputs
        embedded = low_back(low(jnp.dot(patch_v.T, weight_v, precision=HIGH)))
        kv_low = low_back(low(jnp.dot(embedded, kv_weight, precision=HIGH)))
        var_scores = lax.optimization_barrier(jnp.sum((kv_low[:, :D] * agg_query).reshape(SEQ, HEADS, head_dim), axis=-1)) * score_scale
        return (var_scores, kv_low[:, D:])
    var_scores, var_values = lax.map(jax.checkpoint(embed_one), (patches, embed_weight))
    var_valid = (var_mask == 1)[:, None, None]
    highest = lax.optimization_barrier(jnp.max(jnp.where(var_valid, var_scores, NEG_BIG), axis=0))
    exponent = jnp.where(var_valid, jnp.exp(var_scores - highest), 0.0)
    var_probs = exponent / lax.optimization_barrier(jnp.sum(exponent, axis=0))
    agg = jnp.einsum('vsh,vshd->shd', var_probs, var_values.reshape(VARS, SEQ, HEADS, head_dim), precision=HIGH).reshape(SEQ, D)
    agg = low_back(low(agg))
    residual = low_back(jnp.dot(agg, agg_weight, precision=HIGH))
    cond_low = low(jax.nn.silu(cond_vec))
    key_live = jnp.arange(SEQ) < length
    for layer_idx in range(LAYERS):
        ada_weight, ada_bias, qkv_weight, proj_weight, up_weight, down_weight = weights[4 + 6 * layer_idx:10 + 6 * layer_idx]
        modulation = (jnp.dot(cond_low, ada_weight, precision=HIGH) + ada_bias).reshape(6, D)
        hidden_one = low(layer_norm(residual) * (1.0 + modulation[1]) + modulation[0])
        qkv = low_back(low(jnp.dot(hidden_one, qkv_weight, precision=HIGH)))
        queries = qkv[:, :D].reshape(SEQ, HEADS, head_dim)
        keys = qkv[:, D:2 * D].reshape(SEQ, HEADS, head_dim)
        values = qkv[:, 2 * D:].reshape(SEQ, HEADS, head_dim)
        scores = low_back(jnp.einsum('qhd,khd->hqk', queries, keys, precision=HIGH) * score_scale)
        scores = jnp.where(key_live[None, None, :], scores, NEG_BIG)
        highest = lax.optimization_barrier(jnp.max(scores, axis=-1, keepdims=True))
        exponent = jnp.exp(scores - highest)
        probs_low = low(exponent / lax.optimization_barrier(jnp.sum(exponent, axis=-1, keepdims=True)))
        attended = jnp.einsum('hqk,khd->qhd', probs_low, values, precision=HIGH).reshape(SEQ, D)
        attended = low_back(low(attended))
        branch_one = low_back(jnp.dot(attended, proj_weight, precision=HIGH))
        middle = residual + modulation[2] * branch_one
        hidden_two = low(layer_norm(middle) * (1.0 + modulation[4]) + modulation[3])
        pre_act = low_back(jnp.dot(hidden_two, up_weight, precision=HIGH))
        act_low = low(jax.nn.gelu(pre_act, approximate=True))
        branch_two = low_back(jnp.dot(act_low, down_weight, precision=HIGH))
        residual = middle + modulation[5] * branch_two
    return residual

def reference(pixels, var_mask, lengths, condition, cotangent, master, moment_one, moment_two):
    weights = [low(segment) for segment in unpack(master)]
    patches_all = jnp.transpose(pixels.astype(jnp.float32), (2, 0, 1, 3))

    def one_group(totals, inputs):
        patches, length, cond_vec, cot_rows = inputs

        def forward(weight_list, patch_arr):
            return forward_group(weight_list, patch_arr, var_mask, length, cond_vec)
        result, pullback = jax.vjp(forward, weights, patches)
        grad_weights, grad_patches = pullback(cot_rows)
        return ([running + fresh for running, fresh in zip(totals, grad_weights)], (result, grad_patches))
    zero_list = [jnp.zeros_like(segment) for segment in weights]
    totals, (outputs, patch_grads) = lax.scan(one_group, zero_list, (patches_all, lengths, condition.astype(jnp.float32), cotangent))
    grads = pack(totals)
    grad_norm = jnp.sqrt(jnp.sum(grads * grads))
    clip_limit = CLIP_COEF * math.sqrt(PARAMS * TOKENS)
    clipped = grads * (clip_limit / jnp.maximum(grad_norm, clip_limit))
    new_one = BETA_ONE * moment_one + (1.0 - BETA_ONE) * clipped
    new_two = BETA_TWO * moment_two + (1.0 - BETA_TWO) * clipped * clipped
    ratio = new_one / (1.0 - BETA_ONE ** STEP) / (jnp.sqrt(new_two / (1.0 - BETA_TWO ** STEP)) + ADAM_EPS)
    new_master = master - LEARN_RATE * (ratio + WEIGHT_DECAY * master)
    pixel_grad = jnp.transpose(patch_grads, (1, 2, 0, 3))
    return (outputs, pixel_grad, grad_norm, new_master, new_one, new_two, new_master.astype(jnp.bfloat16))
```

```python
import functools
import math

import jax
import jax.numpy as jnp
from jax import lax
from jax.experimental import pallas as pl
from jax.experimental.pallas import tpu as pltpu
from jax.sharding import PartitionSpec as P

D = 384
HEADS = 6
HEAD_DIM = D // HEADS
FF = 1536
VARS = 72
PIX = 4
LAYERS = 2
STEP = 3
PARAMS = 5866368

NEG_BIG = -1e30
NORM_EPS = 1e-06
CLIP_COEF = 0.005
LEARN_RATE = 0.06
WEIGHT_DECAY = 0.1
ADAM_EPS = 1e-08
BETA_ONE = 0.5
BETA_TWO = 0.5
SCORE_SCALE = HEAD_DIM ** (-0.5)

LANES = 128
DB = D // LANES
VP = VARS * PIX
ADA_LINES = 6 * D * D // LANES
BIAS_LINES = 6 * DB
QKV_LINES = 3 * D * D // LANES
PROJ_LINES = D * D // LANES
FF_LINES = D * FF // LANES
EMBED_LINES = VP * DB
KV_LINES = 2 * D * D // LANES
HEAD_LINES = EMBED_LINES + DB + KV_LINES + PROJ_LINES
LAYER_LINES = ADA_LINES + BIAS_LINES + QKV_LINES + PROJ_LINES + 2 * FF_LINES

bf16 = jnp.bfloat16
f32 = jnp.float32


def down16(value):
    return value // 16 * 16


def up16(value):
    return (value + 15) // 16 * 16


def nn(left, right):
    return lax.dot_general(left, right, (((1,), (0,)), ((), ())), preferred_element_type=f32)


def nt(left, right):
    return lax.dot_general(left, right, (((1,), (1,)), ((), ())), preferred_element_type=f32)


def tn(left, right):
    return lax.dot_general(left, right, (((0,), (0,)), ((), ())), preferred_element_type=f32)


def nn_f32(left, right, dims):
    return lax.dot_general(
        left,
        right,
        (dims, ((), ())),
        preferred_element_type=f32,
        precision=lax.Precision.HIGHEST,
    )


VM = pl.BlockSpec(memory_space=pltpu.VMEM)
SM = pl.BlockSpec(memory_space=pltpu.SMEM)
ANY = pl.BlockSpec(memory_space=pl.ANY)


def run(kernel, name, outs, ins, in_specs=None, scratch=(), flops=0, out_specs=None, vmem=32):
    if in_specs is None:
        in_specs = [VM] * len(ins)
    nbytes = sum(math.prod(o.shape) * o.dtype.itemsize for o in outs)
    nbytes += sum(math.prod(i.shape) * i.dtype.itemsize for i in ins)
    return pl.pallas_call(
        kernel,
        name=name,
        out_shape=outs,
        in_specs=in_specs,
        out_specs=out_specs or [VM] * len(outs),
        scratch_shapes=list(scratch),
        cost_estimate=pl.CostEstimate(flops=flops, bytes_accessed=nbytes, transcendentals=0),
        compiler_params=pltpu.CompilerParams(vmem_limit_bytes=vmem * 2**20),
    )(*ins)


def shape(dims, dtype):
    return jax.ShapeDtypeStruct(dims, dtype)


def mod_row(ref, index):
    return jnp.concatenate(
        [ref[DB * index + c : DB * index + c + 1, :] for c in range(DB)], axis=1
    )


def norm_stats(values):
    centered = values - jnp.mean(values, axis=-1, keepdims=True)
    inverse = lax.rsqrt(jnp.mean(centered * centered, axis=-1, keepdims=True) + NORM_EPS)
    return centered * inverse, inverse


def norm_back(grad_normed, normed, inverse):
    mean_grad = jnp.mean(grad_normed, axis=-1, keepdims=True)
    mean_cross = jnp.mean(grad_normed * normed, axis=-1, keepdims=True)
    return inverse * (grad_normed - mean_grad - normed * mean_cross)


def lane_half(shape_):
    return lax.broadcasted_iota(jnp.int32, shape_, 1) < HEAD_DIM


def half_of(pair, half):
    first = lane_half(pair.shape)
    keep = first if half == 0 else jnp.logical_not(first)
    return jnp.where(keep, pair, jnp.zeros_like(pair))


def put_row(ref, index, row):
    for c in range(DB):
        ref[DB * index + c : DB * index + c + 1, :] = row[:, c * LANES : (c + 1) * LANES]


def narrow_lines(src, count, dst):
    step = 512
    whole = count // step

    def body(i, carry):
        row = pl.multiple_of(i * step, step)
        dst[pl.ds(row, step), :] = src[pl.ds(row, step), :].astype(bf16)
        return carry

    if whole:
        lax.fori_loop(0, whole, body, 0)
    rest = count - whole * step
    if rest:
        dst[whole * step : count, :] = src[whole * step : count, :].astype(bf16)


def unpack(lines, start, rows, blocks, out):
    for c in range(blocks):
        out[:, c * LANES : (c + 1) * LANES] = lines[
            pl.ds(start + c, rows, stride=blocks), :
        ].astype(bf16)


class Source:
    def __init__(self, arrays, specs, planned):
        self.arrays = arrays
        self.specs = specs
        self.planned = planned

    def span(self, start, end):
        if not self.planned:
            return down16(start), up16(end)
        return start // HALF * HALF, -(-end // HALF) * HALF

    def load(self, refs, base, lines):
        if not self.planned:
            lines[...] = refs[0][base : base + lines.shape[0], :].astype(f32)
            return
        table = refs[0]
        starts = [o * 2 * HALF + h * HALF for o, h in ENTRIES]
        first = starts.index(base)
        count = lines.shape[0] // HALF
        assert starts[first : first + count] == [base + i * HALF for i in range(count)]

        def body(index, carry):
            code = table[first + index]
            place = code % 4
            at = pl.multiple_of(index * HALF, 16)
            for k in range(12):

                @pl.when(code // 4 == k)
                def copy_block(k=k):
                    lines[pl.ds(at, HALF), :] = refs[1 + k][place].astype(f32)

            return carry

        lax.fori_loop(0, count, body, 0)


def ada_kernel(shard_lines, place, shard, cond_all, spread, column, table, partial, hot):
    line = place[0] * shard_lines + lax.broadcasted_iota(jnp.int32, (shard_lines, 1), 0)
    feature = lax.broadcasted_iota(jnp.int32, (1, D), 1)
    target = jnp.full((shard_lines, 1), -1, jnp.int32)
    is_bias = jnp.zeros((shard_lines, 1), jnp.int32)
    rank = jnp.full((shard_lines, 1), -1, jnp.int32)
    for layer in range(LAYERS):
        begin = HEAD_LINES + layer * LAYER_LINES
        here = jnp.logical_and(line >= begin, line < begin + ADA_LINES)
        rank = jnp.where(here, line - begin, rank)
        target = jnp.where(here, layer * BIAS_LINES, target)
        bias = jnp.logical_and(
            line >= begin + ADA_LINES, line < begin + ADA_LINES + BIAS_LINES
        )
        target = jnp.where(bias, layer * BIAS_LINES + line - begin - ADA_LINES, target)
        is_bias = jnp.where(bias, 1, is_bias)
    passed = rank >= (feature + 1) * BIAS_LINES
    row = jnp.sum(passed.astype(f32), axis=1, keepdims=True).astype(jnp.int32)
    hot[...] = jnp.where(
        jnp.logical_and(rank >= 0, row == feature), 1.0, 0.0
    ).astype(bf16)
    target = jnp.where(rank >= 0, target + rank - row * BIAS_LINES, target)
    factors = nt(hot[...], cond_all[...])
    factors = nn(factors.astype(bf16), spread[...])
    factors = jnp.where(is_bias > 0, 1.0, factors)
    table[...] = jnp.where(target == column[...], factors, 0.0).astype(bf16)
    partial[...] = tn(table[...], shard[...])


def copy_lines(src, start, count, dst, at):
    step = 512
    whole = count // step

    def body(i, carry):
        row = pl.multiple_of(i * step, step)
        dst[pl.ds(at + row, step), :] = src[pl.ds(start + row, step), :]
        return carry

    if whole:
        lax.fori_loop(0, whole, body, 0)
    rest = count - whole * step
    if rest:
        dst[at + whole * step : at + count, :] = src[start + whole * step : start + count, :]


def pack_kernel(meta, table, *refs):
    sections = refs[: len(meta)]
    targets = refs[len(meta) : len(meta) + 6]
    lines = refs[len(meta) + 6]
    end = 0
    tile = None
    for i, (base, size) in enumerate(meta):
        if base > end:
            lines[end:base, :] = jnp.zeros((base - end, LANES), bf16)
        copy_lines(sections[i], 0, size, lines, base)
        if base < end:
            lines[base:end, :] = lines[base:end, :] + tile
        tile = sections[i][size - 16 : size, :]
        end = base + size
    lines[end:, :] = jnp.zeros((lines.shape[0] - end, LANES), bf16)

    def first_line(index):
        number = jnp.where(index < 7, index, jnp.where(index < 28, index + 8, index + 16))
        return number * HALF

    def body(index, carry):
        code = table[index]
        at = pl.multiple_of(first_line(index), 16)
        for k, target in enumerate(targets):

            @pl.when(code // 8 == k)
            def copy_block(target=target):
                target[code % 8] = lines[pl.ds(at, HALF), :]

        return carry

    lax.fori_loop(0, len(ENTRIES), body, 0)


def agg_fwd_kernel(source, *refs):
    pieces = refs[: len(source.arrays)]
    (
        planes, mod,
        res, hid, agg_low, probs, w, u, e, kvw, aggw, query, pix,
        lines, e32, mask,
    ) = refs[len(source.arrays) :]
    source.load(pieces, 0, lines)
    for p in range(PIX):
        for c in range(DB):
            e32[p * VARS : (p + 1) * VARS, c * LANES : (c + 1) * LANES] = lines[
                pl.ds(p * DB + c, VARS, stride=PIX * DB), :
            ]
    e[...] = e32[...].astype(bf16)
    query[...] = jnp.concatenate(
        [lines[EMBED_LINES + c : EMBED_LINES + c + 1, :] for c in range(DB)], axis=1
    )
    unpack(lines, EMBED_LINES + DB, D, 2 * DB, kvw)
    unpack(lines, EMBED_LINES + DB + KV_LINES, D, DB, aggw)
    w[...] = nn(e[...], kvw[...])
    lane = lax.broadcasted_iota(jnp.int32, (VP, LANES), 1)
    table = jnp.zeros((VP, LANES), f32)
    for h in range(HEADS):
        at = h // 2 * LANES
        prod = w[:, at : at + LANES] * query[:, at : at + LANES]
        total = jnp.sum(half_of(prod, h % 2), axis=1, keepdims=True) * SCORE_SCALE
        table = jnp.where(lane == h, total, table)
    u[...] = table
    count = planes.shape[2]
    for b in range(planes.shape[0]):
        for p in range(PIX):
            pix[p, b * count : (b + 1) * count, :] = planes[b, p].astype(f32)
        mask[b * count : (b + 1) * count, :] = planes[b, PIX, :, :LANES].astype(f32)
    live = mask[:, :1] > 0.0
    rows = pix.shape[2]
    for pair in range(HEADS // 2):
        pieces = []
        at = pair * LANES
        for half in range(2):
            h = pair * 2 + half
            scores = jnp.zeros((VARS, rows), f32)
            for p in range(PIX):
                scores += pix[p] * u[p * VARS : (p + 1) * VARS, h : h + 1]
            scores = jnp.where(live, scores, NEG_BIG)
            highest = jnp.max(scores, axis=0, keepdims=True)
            exponent = jnp.where(live, jnp.exp(scores - highest), 0.0)
            prob = exponent / jnp.sum(exponent, axis=0, keepdims=True)
            probs[h] = prob
            weighted = jnp.concatenate([pix[p] * prob for p in range(PIX)], axis=0)
            pieces.append(nn_f32(weighted, w[:, D + at : D + at + LANES], ((0,), (0,))))
        both = jnp.where(lane_half(pieces[0].shape), pieces[0], pieces[1])
        agg_low[:, at : at + LANES] = both.astype(bf16)
    residual = nn(agg_low[...], aggw[...])
    res[...] = residual
    normed, unused = norm_stats(residual)
    hid[...] = (normed * (1.0 + mod_row(mod, 1)) + mod_row(mod, 0)).astype(bf16)


def agg_bwd_kernel(
    go, agg_low, probs, w, u, e, kvw, aggw, query, pix,
    planes, sec,
    sec32, gv, gk, pixg,
):
    rows = pix.shape[2]
    grad_res = go[...].astype(bf16)
    agg_grad = tn(agg_low[...], grad_res)
    start = EMBED_LINES + DB + KV_LINES
    for c in range(DB):
        sec32[pl.ds(start + c, D, stride=DB), :] = agg_grad[:, c * LANES : (c + 1) * LANES]
    grad_agg = nt(grad_res, aggw[...]).astype(bf16)
    first = lane_half((VP, LANES))
    pixel_sum = [jnp.zeros((VARS, rows), f32) for p in range(PIX)]
    for p in range(PIX):
        pixg[p] = pixel_sum[p]
    for pair in range(HEADS // 2):
        at = pair * LANES
        ga_pair = grad_agg[:, at : at + LANES]
        w_pair = w[:, D + at : D + at + LANES]
        value_parts = []
        key_parts = []
        for half in range(2):
            h = pair * 2 + half
            prob = probs[h]
            ga_half = half_of(ga_pair, half)
            back = nn_f32(w_pair, ga_half.astype(f32), ((1,), (1,)))
            grad_probs = jnp.zeros((VARS, rows), f32)
            for p in range(PIX):
                grad_probs += pix[p] * back[p * VARS : (p + 1) * VARS, :]
            inner = jnp.sum(prob * grad_probs, axis=0, keepdims=True)
            grad_scores = prob * (grad_probs - inner)
            sums = []
            for p in range(PIX):
                here = slice(p * VARS, (p + 1) * VARS)
                pixg[p] += grad_scores * u[here, h : h + 1] + prob * back[here, :]
                sums.append(jnp.sum(pix[p] * grad_scores, axis=1, keepdims=True))
            key_parts.append(jnp.concatenate(sums, axis=0) * SCORE_SCALE)
            weighted = jnp.concatenate([pix[p] * prob for p in range(PIX)], axis=0)
            value_parts.append(nn(weighted.astype(bf16), ga_half))
        gv[:, at : at + LANES] = jnp.where(first, value_parts[0], value_parts[1])
        gk[:, at : at + LANES] = jnp.where(first, key_parts[0], key_parts[1])
    count = planes.shape[2]
    for b in range(planes.shape[0]):
        for p in range(PIX):
            planes[b, p] = pixg[p, b * count : (b + 1) * count, :]
    query_grad = jnp.sum(gk[...] * w[:, :D], axis=0, keepdims=True)
    for c in range(DB):
        sec32[EMBED_LINES + c : EMBED_LINES + c + 1, :] = query_grad[:, c * LANES : (c + 1) * LANES]
    grad_kv = jnp.concatenate([gk[...] * query[...], gv[...]], axis=1).astype(bf16)
    kv_grad = tn(e[...], grad_kv)
    start = EMBED_LINES + DB
    for c in range(2 * DB):
        sec32[pl.ds(start + c, D, stride=2 * DB), :] = kv_grad[:, c * LANES : (c + 1) * LANES]
    embed_grad = nt(grad_kv, kvw[...])
    for p in range(PIX):
        for c in range(DB):
            sec32[pl.ds(p * DB + c, VARS, stride=PIX * DB), :] = embed_grad[
                p * VARS : (p + 1) * VARS, c * LANES : (c + 1) * LANES
            ]
    tail = up16(HEAD_LINES) - HEAD_LINES
    sec32[HEAD_LINES:, :] = jnp.zeros((tail, LANES), f32)
    narrow_lines(sec32, up16(HEAD_LINES), sec)


def unpack_kernel(source, base, start, *refs):
    pieces = refs[: len(source.arrays)]
    qkvw, projw, upw, downw, lines = refs[len(source.arrays) :]
    source.load(pieces, base, lines)
    start = start - base
    unpack(lines, start, D, 3 * DB, qkvw)
    start += QKV_LINES
    unpack(lines, start, D, DB, projw)
    start += PROJ_LINES
    unpack(lines, start, D, FF // LANES, upw)
    start += FF_LINES
    unpack(lines, start, FF, DB, downw)


def gelu_parts(value):
    scale = math.sqrt(2.0 / math.pi)
    square = value * value
    tanh = jnp.tanh(scale * (value + 0.044715 * value * square))
    half = 0.5 * (1.0 + tanh)
    slope = half + 0.5 * value * (1.0 - tanh * tanh) * scale * (1.0 + 3.0 * 0.044715 * square)
    return value * half, slope


def layer_fwd_kernel(
    block_count, limits, *refs
):
    hidden = refs[:block_count]
    (res, mod, mod_next, qkvw, projw, upw, downw) = refs[block_count : block_count + 7]
    (qkv, att, lse, b1, mid, pre, b2, res_next, hid_next, h_low, a_low) = refs[block_count + 7 :]
    length = limits[0]
    mine = limits[1]
    rows = res.shape[0]
    seq_len = block_count * rows
    for rel in range(block_count):
        at = pl.multiple_of((mine ^ rel) * rows, rows)
        qkv[pl.ds(at, rows), :] = nn(hidden[rel][...], qkvw[...]).astype(bf16)
    position = lax.broadcasted_iota(jnp.int32, (1, seq_len), 1)
    bias = jnp.where(position < length, 0.0, NEG_BIG)
    own = pl.ds(pl.multiple_of(mine * rows, rows), rows)
    first = lane_half((rows, LANES))
    lane = lax.broadcasted_iota(jnp.int32, (rows, LANES), 1)
    lse[...] = jnp.zeros((rows, LANES), f32)

    def attend(pair, carry):
        at, k_at, v_at = (pl.ds(pl.multiple_of(pair * LANES + i * D, LANES), LANES) for i in range(3))
        query = qkv[own, at] * SCORE_SCALE
        keys = qkv[:, k_at]
        values = qkv[:, v_at]
        parts = []
        for half in range(2):
            scores = nt(half_of(query, half), keys) + bias
            highest = jnp.max(scores, axis=1, keepdims=True)
            exponent = jnp.exp(scores - highest)
            total = jnp.sum(exponent, axis=1, keepdims=True)
            prob = (exponent * (1.0 / total)).astype(bf16)
            parts.append(nn(prob, values))
            lse[...] = jnp.where(lane == pair * 2 + half, highest + jnp.log(total), lse[...])
        att[:, at] = jnp.where(first, parts[0], parts[1])
        return carry

    lax.fori_loop(0, HEADS // 2, attend, 0)
    branch_one = nn(att[...].astype(bf16), projw[...])
    b1[...] = branch_one
    middle = res[...] + mod_row(mod, 2) * branch_one
    mid[...] = middle
    normed, unused = norm_stats(middle)
    h_low[...] = (normed * (1.0 + mod_row(mod, 4)) + mod_row(mod, 3)).astype(bf16)
    pre[...] = nn(h_low[...], upw[...])
    a_low[...] = gelu_parts(pre[...])[0].astype(bf16)
    branch_two = nn(a_low[...], downw[...])
    b2[...] = branch_two
    result = mid[...] + mod_row(mod, 5) * branch_two
    res_next[...] = result
    normed, unused = norm_stats(result)
    hid_next[...] = (normed * (1.0 + mod_row(mod_next, 1)) + mod_row(mod_next, 0)).astype(bf16)


def mlp_bwd_kernel(
    go, mod, pre, mid, b1, b2, att, lse, upw, downw, projw,
    gmid, ga_ext, delta, sums, act_low, gb2_low, h2_low, gp_low, gb1_low,
):
    rows = go.shape[0]
    grad_out = go[...]
    sums[...] = jnp.zeros(sums.shape, f32)
    put_row(sums, 5, jnp.sum(grad_out * b2[...], axis=0, keepdims=True))
    gb2_low[...] = (mod_row(mod, 5) * grad_out).astype(bf16)
    grad_act = nt(gb2_low[...], downw[...])
    act, slope = gelu_parts(pre[...])
    act_low[...] = act.astype(bf16)
    gp_low[...] = (grad_act * slope).astype(bf16)
    grad_hidden = nt(gp_low[...], upw[...])
    normed, inverse = norm_stats(mid[...])
    scale = 1.0 + mod_row(mod, 4)
    h2_low[...] = (normed * scale + mod_row(mod, 3)).astype(bf16)
    put_row(sums, 3, jnp.sum(grad_hidden, axis=0, keepdims=True))
    put_row(sums, 4, jnp.sum(grad_hidden * normed, axis=0, keepdims=True))
    grad_mid = grad_out + norm_back(grad_hidden * scale, normed, inverse)
    gmid[...] = grad_mid
    put_row(sums, 2, jnp.sum(grad_mid * b1[...], axis=0, keepdims=True))
    gb1_low[...] = (mod_row(mod, 2) * grad_mid).astype(bf16)
    grad_att = nt(gb1_low[...], projw[...]).astype(bf16)
    ga_ext[:rows, :] = grad_att
    lane = lax.broadcasted_iota(jnp.int32, (rows, LANES), 1)
    table = jnp.zeros((rows, LANES), f32)
    for h in range(HEADS):
        at = h // 2 * LANES
        prod = grad_att[:, at : at + LANES].astype(f32) * att[:, at : at + LANES]
        total = jnp.sum(half_of(prod, h % 2), axis=1, keepdims=True)
        table = jnp.where(lane == h, total, table)
    delta[...] = table
    both = jnp.where(lane < 8, lse[...], pltpu.roll(table, 8, 1))
    stats = jnp.transpose(both)[:16, :]
    high = stats.astype(bf16)
    low = (stats - high.astype(f32)).astype(bf16)
    ga_ext[rows:, :] = jnp.zeros((32, D), bf16)
    ga_ext[rows : rows + 16, :rows] = high
    ga_ext[rows + 16 : rows + 32, :rows] = low


def mlp_grads_kernel(shift, act_low, gb2_low, h2_low, gp_low, att, gb1_low, sec, sec32):
    lead = jnp.zeros((16, LANES), f32)
    sec32[0:16, :] = lead
    sec32[sec32.shape[0] - 16 :, :] = lead
    start = shift
    proj = tn(att[...].astype(bf16), gb1_low[...])
    for c in range(DB):
        sec32[pl.ds(start + c, D, stride=DB), :] = proj[:, c * LANES : (c + 1) * LANES]
    start += PROJ_LINES
    width = FF // LANES
    for c in range(0, width, 2):
        part = tn(h2_low[...], gp_low[:, c * LANES : (c + 2) * LANES])
        for k in range(2):
            sec32[pl.ds(start + c + k, D, stride=width), :] = part[
                :, k * LANES : (k + 1) * LANES
            ]
    start += FF_LINES
    for r in range(0, FF, D):
        part = tn(act_low[:, r : r + D], gb2_low[...])
        for c in range(DB):
            sec32[pl.ds(start + r * DB + c, D, stride=DB), :] = part[
                :, c * LANES : (c + 1) * LANES
            ]
    narrow_lines(sec32, sec32.shape[0], sec)


def query_bwd_kernel(limits, qkv, ga_ext, lse, delta, gq):
    length = limits[0]
    mine = limits[1]
    rows = lse.shape[0]
    seq_len = qkv.shape[0]
    position = lax.broadcasted_iota(jnp.int32, (1, seq_len), 1)
    bias = jnp.where(position < length, 0.0, NEG_BIG)
    own = pl.ds(pl.multiple_of(mine * rows, rows), rows)
    first = lane_half((rows, LANES))
    lane = lax.broadcasted_iota(jnp.int32, (rows, LANES), 1)

    def column(ref, index):
        return jnp.sum(jnp.where(lane == index, ref[...], 0.0), axis=1, keepdims=True)

    def one_pair(pair, carry):
        at, k_at, v_at = (pl.ds(pl.multiple_of(pair * LANES + i * D, LANES), LANES) for i in range(3))
        query = qkv[own, at] * SCORE_SCALE
        keys = qkv[:, k_at]
        values = qkv[:, v_at]
        grad_pair = ga_ext[:rows, at]
        parts = []
        for half in range(2):
            h = pair * 2 + half
            scores = nt(half_of(query, half), keys) + bias
            prob = jnp.exp(scores - column(lse, h))
            grad_prob = nt(half_of(grad_pair, half), values)
            grad_score = (prob * (grad_prob - column(delta, h))).astype(bf16)
            parts.append(nn(grad_score, keys) * SCORE_SCALE)
        gq[:, at] = jnp.where(first, parts[0], parts[1]).astype(bf16)
        return carry

    lax.fori_loop(0, HEADS // 2, one_pair, 0)


def keys_bwd_kernel(block_count, limits, *refs):
    pieces = refs[:block_count]
    (qkv, gq, res, mod, qkvw, gmid) = refs[block_count : block_count + 6]
    (gqkv, go_prev, sums, stats) = refs[block_count + 6 :]
    length = limits[0]
    mine = limits[1]
    rows = res.shape[0]
    own = pl.ds(pl.multiple_of(mine * rows, rows), rows)
    position = mine * rows + lax.broadcasted_iota(jnp.int32, (rows, 1), 0)
    bias = jnp.where(position < length, 0.0, NEG_BIG)
    first = lane_half((rows, LANES))
    for rel in range(block_count):
        both = pieces[rel][rows : rows + 32, :rows].astype(f32)
        stats[rel] = both[:16, :] + both[16:, :]
    gqkv[:, :D] = gq[...]

    def one_pair(pair, carry):
        at, k_at, v_at = (pl.ds(pl.multiple_of(pair * LANES + i * D, LANES), LANES) for i in range(3))
        keys = qkv[own, k_at] * SCORE_SCALE
        values = qkv[own, v_at]
        key_parts = []
        value_parts = []
        for half in range(2):
            h = pair * 2 + half
            key_half = half_of(keys, half)
            value_half = half_of(values, half)
            key_sum = jnp.zeros((rows, LANES), f32)
            value_sum = jnp.zeros((rows, LANES), f32)
            for rel in range(block_count):
                there = pl.ds(pl.multiple_of((mine ^ rel) * rows, rows), rows)
                query = qkv[there, at]
                grad_pair = pieces[rel][:rows, at]
                scores = nt(key_half, query) + bias
                prob = jnp.exp(scores - stats[rel, pl.ds(h, 1), :])
                grad_prob = nt(value_half, grad_pair)
                grad_score = (prob * (grad_prob - stats[rel, pl.ds(8 + h, 1), :])).astype(bf16)
                key_sum += nn(grad_score, query)
                value_sum += nn(prob.astype(bf16), grad_pair)
            key_parts.append(key_sum * SCORE_SCALE)
            value_parts.append(value_sum)
        gqkv[:, k_at] = jnp.where(first, key_parts[0], key_parts[1]).astype(bf16)
        gqkv[:, v_at] = jnp.where(first, value_parts[0], value_parts[1]).astype(bf16)
        return carry

    lax.fori_loop(0, HEADS // 2, one_pair, 0)
    grad_hidden = nt(gqkv[...], qkvw[...])
    normed, inverse = norm_stats(res[...])
    sums[...] = jnp.zeros(sums.shape, f32)
    put_row(sums, 0, jnp.sum(grad_hidden, axis=0, keepdims=True))
    put_row(sums, 1, jnp.sum(grad_hidden * normed, axis=0, keepdims=True))
    scale = 1.0 + mod_row(mod, 1)
    go_prev[...] = gmid[...] + norm_back(grad_hidden * scale, normed, inverse)


def qkv_grads_kernel(shift, hidden, gqkv, sec, sec32):
    sec32[0:16, :] = jnp.zeros((16, LANES), f32)
    sec32[sec32.shape[0] - 16 :, :] = jnp.zeros((16, LANES), f32)
    width = 3 * DB
    for c in range(0, width, DB):
        part = tn(hidden[...], gqkv[:, c * LANES : (c + DB) * LANES])
        for k in range(DB):
            sec32[pl.ds(shift + c + k, D, stride=width), :] = part[:, k * LANES : (k + 1) * LANES]
    narrow_lines(sec32, sec32.shape[0], sec)


def axis_dims(axis, count):
    dims = []
    for bit in range((count - 1).bit_length()):
        dims.append((axis, [i ^ (1 << bit) for i in range(count)], [i >> bit & 1 for i in range(count)]))
    return dims


def together(values):
    return lax.optimization_barrier(values)


def total_of(parts, begin, end):
    return sum(part[begin:end].astype(f32) for part in parts)


class Cube:
    def __init__(self, var_count, dp_count):
        self.dp_count = dp_count
        self.owners = var_count * dp_count
        var_dims = axis_dims("var", var_count)
        self.core = var_dims[0]
        self.dims = var_dims[1:] + axis_dims("dp", dp_count)

    def partner(self, owner, dim):
        axis, partner, unused = dim
        v, d = divmod(owner, self.dp_count)
        if axis == "var":
            return partner[v] * self.dp_count + d
        return v * self.dp_count + partner[d]

    def bit(self, owner, dim):
        axis, unused, bits = dim
        v, d = divmod(owner, self.dp_count)
        return bits[v] if axis == "var" else bits[d]

    def hop(self, value, *dims, core=None):
        pairs = []
        for owner in range(self.owners):
            other = owner
            for dim in dims:
                other = self.partner(other, dim)
            if core is None or self.bit(owner, self.core) == core:
                pairs.append((owner, other))
        return self.send(value, pairs)

    def send(self, value, pairs):
        return lax.ppermute(value, ("var", "dp"), pairs)

    def mine(self):
        return lax.axis_index("var") * self.dp_count + lax.axis_index("dp")

    def exchange_sum(self, value, groups):
        for group in groups:
            terms = [value]
            for mask in range(1, 2 ** len(group)):
                terms.append(self.hop(value, *[d for i, d in enumerate(group) if mask >> i & 1]))
            while len(terms) > 1:
                terms = [terms[i] + terms[i + 1] for i in range(0, len(terms), 2)]
            value = terms[0]
        return value


PLAN_SHAPE = (4, 8, 1440)
HALF = 720
NEEDED_ZERO = {0: 3, 1: 3, 2: 3, 3: 1, 7: 2, 16: 3, 17: 3, 22: 3, 23: 3}
ENTRIES = (
    [(o, h) for o in (0, 1, 2) for h in (0, 1)]
    + [(3, 0), (7, 1)]
    + [(o, h) for o in range(8, 18) for h in (0, 1)]
    + [(o, h) for o in range(22, 32) for h in (0, 1)]
)


class Plan:
    def __init__(self, cube):
        self.cube = cube
        x, y, step, pair = cube.dims
        self.pair = pair
        self.orders = ((x, y, step), (y, step, x), (step, x, y))
        rows = [self.codes(o) + self.flags(o) for o in range(cube.owners)]
        row = jnp.asarray(rows, jnp.int32)[cube.mine()]
        self.table = row[: len(ENTRIES)]
        self.flag = [row[len(ENTRIES) + i] == 1 for i in range(3)]
        ones = [o for o in range(cube.owners) if cube.bit(o, cube.core)]
        self.ones_pairs = [(o, cube.partner(o, pair)) for o in ones]
        self.zero_pairs = [(o, cube.partner(o, pair)) for o in NEEDED_ZERO]

    def flags(self, device):
        needed = NEEDED_ZERO.get(device, 0)
        return [self.cube.bit(device, self.cube.core), needed & 1, needed >> 1]

    def codes(self, device):
        cube = self.cube
        codes = []
        for owner, half in ENTRIES:
            chunk = 1 + half
            stream = cube.bit(owner, cube.core)
            if stream == 1 and cube.bit(owner, self.pair) == cube.bit(device, self.pair):
                chunk = 0
                stream = 1 - half
            place = 0
            for s, dim in enumerate(self.orders[chunk]):
                place += (cube.bit(owner, dim) ^ cube.bit(device, dim)) << s
            codes.append(chunk * 16 + (stream ^ cube.bit(device, cube.core)) * 8 + place)
        return codes

    def gather(self, shard, shard_zero, early, first_work, late, last_work):
        cube = self.cube
        is_one, own_first, own_second = self.flag
        lower = cube.hop(shard[HALF:], cube.core)
        from_one = cube.send(shard, self.ones_pairs)
        from_zero = cube.send(shard_zero, self.zero_pairs)
        from_one, from_zero, early = together((from_one, from_zero, early))
        first = jnp.where(own_first, shard[:HALF], from_zero[:HALF])
        second = jnp.where(own_second, shard[HALF:], from_zero[HALF:])
        current = [
            jnp.where(is_one, shard[:HALF], lower)[None],
            jnp.where(is_one, from_one[:HALF], first)[None],
            jnp.where(is_one, from_one[HALF:], second)[None],
        ]
        early = first_work(early)
        for step in range(2):
            got = [cube.hop(current[q], self.orders[q][step]) for q in range(3)]
            current = [jnp.concatenate([a, b], axis=0) for a, b in zip(current, got)]
        current, early, late = together((current, early, late))
        last = [cube.hop(current[q], self.orders[q][2]) for q in range(3)]
        other = [cube.hop(value, cube.core) for value in current]
        last, late = together((last, last_work(late)))
        other_last = [cube.hop(value, cube.core) for value in last]
        pieces = [entry for group in zip(current, last, other, other_last) for entry in group]
        return pieces, early, late

    def scatter(self, keep, send, late, work):
        cube = self.cube
        is_one, own_first, own_second = self.flag
        parts = [[a, cube.hop(b, cube.core)] for a, b in zip(keep, send)]
        half = 4
        for step in range(3):
            outs = [total_of(part, half, 2 * half).astype(bf16) for part in parts]
            for q in range(3):
                got = cube.hop(outs[q], self.orders[q][2 - step])
                parts[q] = [part[:half] for part in parts[q]] + [got]
            half //= 2
        first, second, third = (total_of(part, 0, 1)[0] for part in parts)
        both = jnp.concatenate([second, third], axis=0)
        back = [(b, a) for a, b in self.ones_pairs + self.zero_pairs]
        partner = cube.send(both.astype(bf16), back).astype(f32)
        lower = cube.hop(first.astype(bf16), cube.core).astype(f32)
        lower, late = together((lower, late))
        partner, late = together((partner, work(late)))
        one = jnp.concatenate([first, lower], axis=0)
        return jnp.where(is_one, one, both) + partner, late


def flip(value, axis, bit):
    count = lax.axis_size(axis)
    return lax.ppermute(value, axis, [(i, i ^ bit) for i in range(count)])


def gather_blocks(value, extra):
    count = lax.axis_size("var")
    pieces = {0: value}
    bit = count // 2
    while bit:
        got = {r ^ bit: flip(piece, "var", bit) for r, piece in pieces.items()}
        if bit == 2:
            got, extra = together((got, extra))
        pieces.update(got)
        bit //= 2
    return [pieces[r] for r in range(count)], extra


def local(pixels, var_mask, lengths, condition, cotangent, master, moment_one, moment_two):
    var_count = lax.axis_size("var")
    dp_count = lax.axis_size("dp")
    var_index = lax.axis_index("var")
    rows = cotangent.shape[1]
    seq_len = rows * var_count
    local_vars = pixels.shape[0]
    shard_lines = master.shape[0] // LANES
    total_lines = shard_lines * var_count * dp_count

    shard = master.astype(bf16).reshape(shard_lines, LANES)
    present = jnp.where(var_mask == 1, 1.0, 0.0).astype(bf16)
    planes = jnp.concatenate(
        [pixels[:, :, 0, :], jnp.broadcast_to(present[:, None, None], (local_vars, 1, seq_len))],
        axis=1,
    )
    planes = planes.reshape(local_vars, PIX + 1, var_count, rows).transpose(2, 1, 0, 3)

    def spread(values):
        return lax.all_to_all(values, "var", 0, 0, tiled=True)

    cube = Cube(var_count, dp_count)
    planned = (var_count, dp_count, shard_lines) == PLAN_SHAPE
    cond_low = jax.nn.silu(condition.astype(f32)).astype(bf16)
    limits = jnp.stack([lengths[0], var_index.astype(jnp.int32)])
    if planned:
        plan = Plan(cube)
        dp_index = lax.axis_index("dp")
        slots = LAYERS * BIAS_LINES
        x, y, *zs = cube.dims
        every = [[cube.core], [x, y], zs]

        def to_all(value):
            copies = jnp.broadcast_to(value[None], (dp_count,) + value.shape)
            return lax.all_to_all(copies, "dp", 0, 0, tiled=True)

        conds = to_all(cond_low[0].reshape(DB, LANES)).reshape(dp_count, D)
        shard_zero, conds = together((shard, conds))
        of_slot = jnp.arange(dp_count * slots) // slots
        ada_table, partial = run(
            functools.partial(ada_kernel, shard_lines),
            "ada",
            [shape((shard_lines, dp_count * slots), bf16), shape((dp_count * slots, LANES), f32)],
            [
                cube.mine()[None].astype(jnp.int32), shard, conds,
                (jnp.arange(dp_count)[:, None] == of_slot[None, :]).astype(bf16),
                (jnp.arange(dp_count * slots) % slots)[None, :].astype(jnp.int32),
            ],
            [SM] + [VM] * 4,
            [pltpu.VMEM((shard_lines, D), bf16)],
            flops=10**9,
        )
        partial = lax.all_to_all(
            partial.reshape(dp_count, slots, LANES), "dp", 0, 0, tiled=True
        )

        def beside(sums):
            return cube.exchange_sum(sums, [[cube.core], [x]])

        pieces, own, planes = plan.gather(
            shard, shard_zero, jnp.sum(partial, axis=0), beside, planes, spread
        )
        arrays = [plan.table, *pieces]
        specs = [SM] + [VM] * len(pieces)
        mods = [own[layer * BIAS_LINES : (layer + 1) * BIAS_LINES] for layer in range(LAYERS)]
    else:
        planes = spread(planes)
        arrays = [lax.all_gather(shard, ("var", "dp"), axis=0, tiled=True)]
        specs = [VM]
        mods = []
        for layer in range(LAYERS):
            start = HEAD_LINES + layer * LAYER_LINES
            ada = arrays[0][start : start + ADA_LINES].reshape(D, 6 * D)
            bias = arrays[0][start + ADA_LINES : start + ADA_LINES + BIAS_LINES]
            mods.append(
                jnp.dot(cond_low, ada, preferred_element_type=f32).reshape(BIAS_LINES, LANES)
                + bias.astype(f32)
            )
    mods = [jnp.pad(mod, ((0, 24 - BIAS_LINES), (0, 0))) for mod in mods]
    source = Source(arrays, specs, planned)

    begin, end = source.span(0, HEAD_LINES)
    (residual, hidden, agg_low, probs, w, u, e, kvw, aggw, query, pix) = run(
        functools.partial(agg_fwd_kernel, source),
        "agg_fwd",
        [
            shape((rows, D), f32), shape((rows, D), bf16), shape((rows, D), bf16),
            shape((HEADS, VARS, rows), f32), shape((VP, 2 * D), f32), shape((VP, LANES), f32),
            shape((VP, D), bf16), shape((D, 2 * D), bf16), shape((D, D), bf16),
            shape((1, D), f32), shape((PIX, VARS, rows), f32),
        ],
        [*arrays, planes, mods[0]],
        [*specs, VM, VM],
        [
            pltpu.VMEM((end - begin, LANES), f32), pltpu.VMEM((VP, D), f32),
            pltpu.VMEM((VARS, LANES), f32),
        ],
        flops=10**9,
    )

    def unpack_layer(layer):
        start = HEAD_LINES + layer * LAYER_LINES + ADA_LINES + BIAS_LINES
        begin, end = source.span(start, HEAD_LINES + (layer + 1) * LAYER_LINES)
        return run(
            functools.partial(unpack_kernel, source, begin, start),
            f"unpack_{layer}",
            [
                shape((D, 3 * D), bf16), shape((D, D), bf16), shape((D, FF), bf16),
                shape((FF, D), bf16),
            ],
            arrays,
            specs,
            [pltpu.VMEM((end - begin, LANES), f32)],
            flops=10**9,
            vmem=24,
        )

    weights = [None] * LAYERS
    hidden_blocks, weights[0] = gather_blocks(hidden, unpack_layer(0))

    stored = []
    for layer in range(LAYERS):
        qkvw, projw, upw, downw = weights[layer]
        mod = mods[layer]
        mod_next = mods[min(layer + 1, LAYERS - 1)]
        blocks = hidden_blocks
        outs = [
            shape((seq_len, 3 * D), bf16), shape((rows, D), f32), shape((rows, LANES), f32),
            shape((rows, D), f32), shape((rows, D), f32), shape((rows, FF), f32),
            shape((rows, D), f32), shape((rows, D), f32), shape((rows, D), bf16),
        ]
        qkv, att, lse, b1, mid, pre, b2, next_residual, next_hidden = run(
            functools.partial(layer_fwd_kernel, var_count),
            f"layer_fwd_{layer}",
            outs,
            [limits, *blocks, residual, mod, mod_next, qkvw, projw, upw, downw],
            [SM] + [VM] * (var_count + 7),
            [pltpu.VMEM((rows, D), bf16), pltpu.VMEM((rows, FF), bf16)],
            flops=4 * 10**9,
        )
        stored.append((hidden, residual, qkv, att, lse, b1, mid, pre, b2))
        residual, hidden = next_residual, next_hidden
        if layer + 1 < LAYERS:
            hidden_blocks, weights[layer + 1] = gather_blocks(hidden, unpack_layer(layer + 1))
    output = residual

    grad_out = cotangent[0]
    sections = []
    ada_sums = [None] * LAYERS
    for layer in reversed(range(LAYERS)):
        qkvw, projw, upw, downw = weights[layer]
        mod = mods[layer]
        hidden, residual, qkv, att, lse, b1, mid, pre, b2 = stored[layer]
        first_line = HEAD_LINES + layer * LAYER_LINES
        outs = [
            shape((rows, D), f32), shape((rows + 32, D), bf16), shape((rows, LANES), f32),
            shape((24, LANES), f32), shape((rows, FF), bf16), shape((rows, D), bf16),
            shape((rows, D), bf16), shape((rows, FF), bf16), shape((rows, D), bf16),
        ]
        gmid, ga_ext, delta, sums_a, act_low, gb2_low, h2_low, gp_low, gb1_low = run(
            mlp_bwd_kernel,
            f"mlp_bwd_{layer}",
            outs,
            [grad_out, mod, pre, mid, b1, b2, att, lse, upw, downw, projw],
            flops=2 * 10**9,
        )
        (gq,) = run(
            query_bwd_kernel,
            f"query_bwd_{layer}",
            [shape((rows, D), bf16)],
            [limits, qkv, ga_ext, lse, delta],
            [SM] + [VM] * 4,
            flops=4 * 10**9,
        )
        blocks, gq = gather_blocks(ga_ext, gq)
        start = first_line + ADA_LINES + BIAS_LINES + QKV_LINES
        count = up16(start + PROJ_LINES + 2 * FF_LINES) - down16(start)
        (section,) = run(
            functools.partial(mlp_grads_kernel, start - down16(start)),
            f"mlp_grads_{layer}",
            [shape((count, LANES), bf16)],
            [act_low, gb2_low, h2_low, gp_low, att, gb1_low],
            scratch=[pltpu.VMEM((count, LANES), f32)],
            flops=2 * 10**9,
        )
        sections.append((start, PROJ_LINES + 2 * FF_LINES, section))
        gqkv, grad_out, sums_b = run(
            functools.partial(keys_bwd_kernel, var_count),
            f"keys_bwd_{layer}",
            [shape((rows, 3 * D), bf16), shape((rows, D), f32), shape((24, LANES), f32)],
            [limits, *blocks, qkv, gq, residual, mod, qkvw, gmid],
            [SM] + [VM] * (var_count + 6),
            [pltpu.VMEM((var_count, 16, rows), f32)],
            flops=5 * 10**9,
        )
        start = first_line + ADA_LINES + BIAS_LINES
        count = up16(start + QKV_LINES) - down16(start)
        (section,) = run(
            functools.partial(qkv_grads_kernel, start - down16(start)),
            f"qkv_grads_{layer}",
            [shape((count, LANES), bf16)],
            [hidden, gqkv],
            scratch=[pltpu.VMEM((count, LANES), f32)],
            flops=10**9,
        )
        sections.append((start, QKV_LINES, section))
        ada_sums[layer] = (sums_a + sums_b)[:BIAS_LINES]

    pixel_grad, section = run(
        agg_bwd_kernel,
        "agg_bwd",
        [
            shape((var_count, PIX, local_vars, rows), f32),
            shape((up16(HEAD_LINES), LANES), bf16),
        ],
        [grad_out, agg_low, probs, w, u, e, kvw, aggw, query, pix],
        scratch=[
            pltpu.VMEM((up16(HEAD_LINES), LANES), f32), pltpu.VMEM((VP, D), f32),
            pltpu.VMEM((VP, D), f32), pltpu.VMEM((PIX, VARS, rows), f32),
        ],
        flops=10**9,
    )
    sections.append((0, HEAD_LINES, section))
    def unspread(values):
        values = lax.all_to_all(values, "var", 0, 0, tiled=True)
        return values.transpose(2, 1, 0, 3).reshape(local_vars, PIX, seq_len)

    if planned:
        sections.sort(key=lambda entry: entry[0])
        meta = [(down16(start), part.shape[0]) for start, count, part in sections]
        own = cube.exchange_sum(jnp.concatenate(ada_sums, axis=0), [[cube.core], [x]])
        parts, own = together(([s[2] for s in sections], own))
        packed = run(
            functools.partial(pack_kernel, meta),
            "pack",
            [shape((8, HALF, LANES), bf16)] * 6,
            [
                plan.table,
                *parts,
            ],
            [SM] + [VM] * len(sections),
            [pltpu.VMEM((total_lines, LANES), bf16)],
            vmem=16,
        )

        def beside_scatter(values):
            grads, own = values
            return unspread(grads), to_all(own)

        grad_lines, (patch_grads, sums) = plan.scatter(
            packed[::2], packed[1::2], (pixel_grad, own), beside_scatter
        )
        sums = sums.reshape(dp_count * slots, LANES)
        high = sums.astype(bf16)
        low = (sums - high.astype(f32)).astype(bf16)
        ada_lines = nn(ada_table, high) + nn(ada_table, low)
        line = cube.mine() * shard_lines + lax.broadcasted_iota(jnp.int32, (shard_lines, 1), 0)
        for layer in range(LAYERS):
            start = HEAD_LINES + layer * LAYER_LINES
            inside = jnp.logical_and(line >= start, line < start + ADA_LINES + BIAS_LINES)
            grad_lines = jnp.where(inside, ada_lines, grad_lines)
    else:
        patch_grads = unspread(pixel_grad)
        for layer in range(LAYERS):
            start = HEAD_LINES + layer * LAYER_LINES
            outer = cond_low[0].astype(f32)[:, None, None] * ada_sums[layer][None]
            outer = outer.reshape(ADA_LINES, LANES).astype(bf16)
            shift = start - down16(start)
            outer = jnp.concatenate(
                [jnp.zeros((shift, LANES), bf16), outer, ada_sums[layer].astype(bf16)], axis=0
            )
            sections.append((start, ADA_LINES + BIAS_LINES, outer))
        sections.sort(key=lambda entry: entry[0])
        parts = [
            part[start - down16(start) : start - down16(start) + count]
            for start, count, part in sections
        ]
        used = sections[-1][0] + sections[-1][1]
        parts.append(jnp.zeros((total_lines - used, LANES), bf16))
        whole = jnp.concatenate(parts, axis=0)
        grad_lines = lax.psum_scatter(
            whole, ("var", "dp"), scatter_dimension=0, tiled=True
        ).astype(f32)
    grad_shard = grad_lines.reshape(-1)
    squares = jnp.sum(grad_shard * grad_shard)
    if planned:
        squares = cube.exchange_sum(jnp.broadcast_to(squares, (8, LANES)), every)[0, 0]
    else:
        squares = lax.psum(squares, ("var", "dp"))
    grad_norm = jnp.sqrt(squares)
    clip_limit = CLIP_COEF * math.sqrt(PARAMS * seq_len * dp_count)
    clipped = grad_shard * (clip_limit / jnp.maximum(grad_norm, clip_limit))
    new_one = BETA_ONE * moment_one + (1.0 - BETA_ONE) * clipped
    new_two = BETA_TWO * moment_two + (1.0 - BETA_TWO) * clipped * clipped
    ratio = (
        new_one / (1.0 - BETA_ONE**STEP) / (jnp.sqrt(new_two / (1.0 - BETA_TWO**STEP)) + ADAM_EPS)
    )
    new_master = master - LEARN_RATE * (ratio + WEIGHT_DECAY * master)
    return (
        output[None],
        patch_grads[:, :, None, :],
        grad_norm,
        new_master,
        new_one,
        new_two,
        new_master.astype(bf16),
    )


def solution(mesh):
    in_specs = (
        P("var", None, "dp", None),
        P("var"),
        P("dp"),
        P("dp", None),
        P("dp", "var", None),
        P(("var", "dp")),
        P(("var", "dp")),
        P(("var", "dp")),
    )
    out_specs = (
        P("dp", "var", None),
        P("var", None, "dp", None),
        P(),
        P(("var", "dp")),
        P(("var", "dp")),
        P(("var", "dp")),
        P(("var", "dp")),
    )
    return jax.shard_map(local, mesh=mesh, in_specs=in_specs, out_specs=out_specs, check_vma=False)
```

```python
import functools
import math

import jax
import jax.numpy as jnp
from jax import lax
from jax.experimental import pallas as pl
from jax.experimental.pallas import tpu as pltpu
from jax.sharding import PartitionSpec as P

D = 384
HEADS = 6
HEAD_DIM = D // HEADS
FF = 1536
VARS = 72
PIX = 4
LAYERS = 2
STEP = 3
PARAMS = 5866368

NEG_BIG = -1e30
NORM_EPS = 1e-06
CLIP_COEF = 0.005
LEARN_RATE = 0.06
WEIGHT_DECAY = 0.1
ADAM_EPS = 1e-08
BETA_ONE = 0.5
BETA_TWO = 0.5
SCORE_SCALE = HEAD_DIM ** (-0.5)

LANES = 128
DB = D // LANES
VP = VARS * PIX
ADA_LINES = 6 * D * D // LANES
BIAS_LINES = 6 * DB
QKV_LINES = 3 * D * D // LANES
PROJ_LINES = D * D // LANES
FF_LINES = D * FF // LANES
EMBED_LINES = VP * DB
KV_LINES = 2 * D * D // LANES
HEAD_LINES = EMBED_LINES + DB + KV_LINES + PROJ_LINES
LAYER_LINES = ADA_LINES + BIAS_LINES + QKV_LINES + PROJ_LINES + 2 * FF_LINES

bf16 = jnp.bfloat16
f32 = jnp.float32


def down16(value):
    return value // 16 * 16


def up16(value):
    return (value + 15) // 16 * 16


def nn(left, right):
    return lax.dot_general(left, right, (((1,), (0,)), ((), ())), preferred_element_type=f32)


def nt(left, right):
    return lax.dot_general(left, right, (((1,), (1,)), ((), ())), preferred_element_type=f32)


def tn(left, right):
    return lax.dot_general(left, right, (((0,), (0,)), ((), ())), preferred_element_type=f32)


def nn_f32(left, right, dims):
    return lax.dot_general(
        left,
        right,
        (dims, ((), ())),
        preferred_element_type=f32,
        precision=lax.Precision.HIGHEST,
    )


VMEM_MIB = {
    "ada": 14,
    "agg_fwd": 14,
    "unpack": 14,
    "near_attend": 16,
    "layer_fwd": 24,
    "mlp_bwd": 16,
    "query_bwd": 16,
    "mlp_grads": 12,
    "near_keys": 16,
    "keys_bwd": 16,
    "qkv_grads": 10,
    "agg_bwd": 14,
    "pack": 16,
}

VM = pl.BlockSpec(memory_space=pltpu.VMEM)
SM = pl.BlockSpec(memory_space=pltpu.SMEM)
ANY = pl.BlockSpec(memory_space=pl.ANY)


def run(kernel, name, outs, ins, in_specs=None, scratch=(), flops=0, out_specs=None):
    if in_specs is None:
        in_specs = [VM] * len(ins)
    nbytes = sum(math.prod(o.shape) * o.dtype.itemsize for o in outs)
    nbytes += sum(math.prod(i.shape) * i.dtype.itemsize for i in ins)
    return pl.pallas_call(
        kernel,
        name=name,
        out_shape=outs,
        in_specs=in_specs,
        out_specs=out_specs or [VM] * len(outs),
        scratch_shapes=list(scratch),
        cost_estimate=pl.CostEstimate(flops=flops, bytes_accessed=nbytes, transcendentals=0),
        compiler_params=pltpu.CompilerParams(vmem_limit_bytes=VMEM_MIB[name.rstrip("_0123456789")] * 2**20),
    )(*ins)


def shape(dims, dtype):
    return jax.ShapeDtypeStruct(dims, dtype)


def mod_row(ref, index):
    return jnp.concatenate(
        [ref[DB * index + c : DB * index + c + 1, :] for c in range(DB)], axis=1
    )


def norm_stats(values):
    centered = values - jnp.mean(values, axis=-1, keepdims=True)
    inverse = lax.rsqrt(jnp.mean(centered * centered, axis=-1, keepdims=True) + NORM_EPS)
    return centered * inverse, inverse


def norm_back(grad_normed, normed, inverse):
    mean_grad = jnp.mean(grad_normed, axis=-1, keepdims=True)
    mean_cross = jnp.mean(grad_normed * normed, axis=-1, keepdims=True)
    return inverse * (grad_normed - mean_grad - normed * mean_cross)


def lane_half(shape_):
    return lax.broadcasted_iota(jnp.int32, shape_, 1) < HEAD_DIM


def half_of(pair, half):
    first = lane_half(pair.shape)
    keep = first if half == 0 else jnp.logical_not(first)
    return jnp.where(keep, pair, jnp.zeros_like(pair))


def put_row(ref, index, row):
    for c in range(DB):
        ref[DB * index + c : DB * index + c + 1, :] = row[:, c * LANES : (c + 1) * LANES]


def narrow_lines(src, count, dst):
    step = 512
    whole = count // step

    def body(i, carry):
        row = pl.multiple_of(i * step, step)
        dst[pl.ds(row, step), :] = src[pl.ds(row, step), :].astype(bf16)
        return carry

    if whole:
        lax.fori_loop(0, whole, body, 0)
    rest = count - whole * step
    if rest:
        dst[whole * step : count, :] = src[whole * step : count, :].astype(bf16)


def unpack(lines, start, rows, blocks, out):
    for c in range(blocks):
        out[:, c * LANES : (c + 1) * LANES] = lines[
            pl.ds(start + c, rows, stride=blocks), :
        ].astype(bf16)


class Source:
    def __init__(self, arrays, specs, planned):
        self.arrays = arrays
        self.specs = specs
        self.planned = planned

    def span(self, start, end):
        if not self.planned:
            return down16(start), up16(end)
        return start // HALF * HALF, -(-end // HALF) * HALF

    def load(self, refs, base, lines):
        if not self.planned:
            lines[...] = refs[0][base : base + lines.shape[0], :].astype(f32)
            return
        table = refs[0]
        starts = [o * 2 * HALF + h * HALF for o, h in ENTRIES]
        first = starts.index(base)
        count = lines.shape[0] // HALF
        assert starts[first : first + count] == [base + i * HALF for i in range(count)]

        def body(index, carry):
            code = table[first + index]
            place = code % 4
            at = pl.multiple_of(index * HALF, 16)
            for k in range(12):

                @pl.when(code // 4 == k)
                def copy_block(k=k):
                    lines[pl.ds(at, HALF), :] = refs[1 + k][place].astype(f32)

            return carry

        lax.fori_loop(0, count, body, 0)


def ada_kernel(shard_lines, place, shard, cond_all, spread, column, table, partial, hot):
    line = place[0] * shard_lines + lax.broadcasted_iota(jnp.int32, (shard_lines, 1), 0)
    feature = lax.broadcasted_iota(jnp.int32, (1, D), 1)
    target = jnp.full((shard_lines, 1), -1, jnp.int32)
    is_bias = jnp.zeros((shard_lines, 1), jnp.int32)
    rank = jnp.full((shard_lines, 1), -1, jnp.int32)
    for layer in range(LAYERS):
        begin = HEAD_LINES + layer * LAYER_LINES
        here = jnp.logical_and(line >= begin, line < begin + ADA_LINES)
        rank = jnp.where(here, line - begin, rank)
        target = jnp.where(here, layer * BIAS_LINES, target)
        bias = jnp.logical_and(
            line >= begin + ADA_LINES, line < begin + ADA_LINES + BIAS_LINES
        )
        target = jnp.where(bias, layer * BIAS_LINES + line - begin - ADA_LINES, target)
        is_bias = jnp.where(bias, 1, is_bias)
    passed = rank >= (feature + 1) * BIAS_LINES
    row = jnp.sum(passed.astype(f32), axis=1, keepdims=True).astype(jnp.int32)
    hot[...] = jnp.where(
        jnp.logical_and(rank >= 0, row == feature), 1.0, 0.0
    ).astype(bf16)
    target = jnp.where(rank >= 0, target + rank - row * BIAS_LINES, target)
    factors = nt(hot[...], cond_all[...])
    factors = nn(factors.astype(bf16), spread[...])
    factors = jnp.where(is_bias > 0, 1.0, factors)
    table[...] = jnp.where(target == column[...], factors, 0.0).astype(bf16)
    partial[...] = tn(table[...], shard[...])


def copy_lines(src, start, count, dst, at):
    step = 512
    whole = count // step

    def body(i, carry):
        row = pl.multiple_of(i * step, step)
        dst[pl.ds(at + row, step), :] = src[pl.ds(start + row, step), :]
        return carry

    if whole:
        lax.fori_loop(0, whole, body, 0)
    rest = count - whole * step
    if rest:
        dst[at + whole * step : at + count, :] = src[start + whole * step : start + count, :]


def pack_kernel(meta, table, *refs):
    sections = refs[: len(meta)]
    targets = refs[len(meta) : len(meta) + 6]
    lines = refs[len(meta) + 6]
    starts = [o * 2 * HALF + h * HALF for o, h in ENTRIES]
    end = 0
    tile = None
    for i, (base, size) in enumerate(meta):
        entry = max(e for e, start in enumerate(starts) if start <= base)
        base = base - starts[entry] + entry * HALF
        if base > end:
            lines[end:base, :] = jnp.zeros((base - end, LANES), bf16)
        copy_lines(sections[i], 0, size, lines, base)
        if base < end:
            lines[base:end, :] = lines[base:end, :] + tile
        tile = sections[i][size - 16 : size, :]
        end = base + size
    lines[end:, :] = jnp.zeros((lines.shape[0] - end, LANES), bf16)

    def body(index, carry):
        code = table[index]
        at = pl.multiple_of(index * HALF, 16)
        for k, target in enumerate(targets):

            @pl.when(code // 8 == k)
            def copy_block(target=target):
                target[code % 8] = lines[pl.ds(at, HALF), :]

        return carry

    lax.fori_loop(0, len(ENTRIES), body, 0)


def agg_fwd_kernel(source, *refs):
    pieces = refs[: len(source.arrays)]
    (
        planes, mod,
        res, hid, agg_low, probs, w, u, e, kvw, aggw, query, pix,
        lines, e32, mask,
    ) = refs[len(source.arrays) :]
    source.load(pieces, 0, lines)
    for p in range(PIX):
        for c in range(DB):
            e32[p * VARS : (p + 1) * VARS, c * LANES : (c + 1) * LANES] = lines[
                pl.ds(p * DB + c, VARS, stride=PIX * DB), :
            ]
    e[...] = e32[...].astype(bf16)
    query[...] = jnp.concatenate(
        [lines[EMBED_LINES + c : EMBED_LINES + c + 1, :] for c in range(DB)], axis=1
    )
    unpack(lines, EMBED_LINES + DB, D, 2 * DB, kvw)
    unpack(lines, EMBED_LINES + DB + KV_LINES, D, DB, aggw)
    w[...] = nn(e[...], kvw[...])
    lane = lax.broadcasted_iota(jnp.int32, (VP, LANES), 1)
    table = jnp.zeros((VP, LANES), f32)
    for h in range(HEADS):
        at = h // 2 * LANES
        prod = w[:, at : at + LANES] * query[:, at : at + LANES]
        total = jnp.sum(half_of(prod, h % 2), axis=1, keepdims=True) * SCORE_SCALE
        table = jnp.where(lane == h, total, table)
    u[...] = table
    count = planes.shape[2]
    for b in range(planes.shape[0]):
        for p in range(PIX):
            pix[p, b * count : (b + 1) * count, :] = planes[b, p].astype(f32)
        mask[b * count : (b + 1) * count, :] = planes[b, PIX, :, :LANES].astype(f32)
    live = mask[:, :1] > 0.0
    rows = pix.shape[2]
    for pair in range(HEADS // 2):
        pieces = []
        at = pair * LANES
        for half in range(2):
            h = pair * 2 + half
            scores = jnp.zeros((VARS, rows), f32)
            for p in range(PIX):
                scores += pix[p] * u[p * VARS : (p + 1) * VARS, h : h + 1]
            scores = jnp.where(live, scores, NEG_BIG)
            highest = jnp.max(scores, axis=0, keepdims=True)
            exponent = jnp.where(live, jnp.exp(scores - highest), 0.0)
            prob = exponent / jnp.sum(exponent, axis=0, keepdims=True)
            probs[h] = prob
            weighted = jnp.concatenate([pix[p] * prob for p in range(PIX)], axis=0)
            pieces.append(nn_f32(weighted, w[:, D + at : D + at + LANES], ((0,), (0,))))
        both = jnp.where(lane_half(pieces[0].shape), pieces[0], pieces[1])
        agg_low[:, at : at + LANES] = both.astype(bf16)
    residual = nn(agg_low[...], aggw[...])
    res[...] = residual
    normed, unused = norm_stats(residual)
    hid[...] = (normed * (1.0 + mod_row(mod, 1)) + mod_row(mod, 0)).astype(bf16)


def agg_bwd_kernel(
    go, agg_low, probs, w, u, e, kvw, aggw, query, pix,
    planes, sec,
    sec32, gv, gk, pixg,
):
    rows = pix.shape[2]
    grad_res = go[...].astype(bf16)
    agg_grad = tn(agg_low[...], grad_res)
    start = EMBED_LINES + DB + KV_LINES
    for c in range(DB):
        sec32[pl.ds(start + c, D, stride=DB), :] = agg_grad[:, c * LANES : (c + 1) * LANES]
    grad_agg = nt(grad_res, aggw[...]).astype(bf16)
    first = lane_half((VP, LANES))
    pixel_sum = [jnp.zeros((VARS, rows), f32) for p in range(PIX)]
    for p in range(PIX):
        pixg[p] = pixel_sum[p]
    for pair in range(HEADS // 2):
        at = pair * LANES
        ga_pair = grad_agg[:, at : at + LANES]
        w_pair = w[:, D + at : D + at + LANES]
        value_parts = []
        key_parts = []
        for half in range(2):
            h = pair * 2 + half
            prob = probs[h]
            ga_half = half_of(ga_pair, half)
            back = nn_f32(w_pair, ga_half.astype(f32), ((1,), (1,)))
            grad_probs = jnp.zeros((VARS, rows), f32)
            for p in range(PIX):
                grad_probs += pix[p] * back[p * VARS : (p + 1) * VARS, :]
            inner = jnp.sum(prob * grad_probs, axis=0, keepdims=True)
            grad_scores = prob * (grad_probs - inner)
            sums = []
            for p in range(PIX):
                here = slice(p * VARS, (p + 1) * VARS)
                pixg[p] += grad_scores * u[here, h : h + 1] + prob * back[here, :]
                sums.append(jnp.sum(pix[p] * grad_scores, axis=1, keepdims=True))
            key_parts.append(jnp.concatenate(sums, axis=0) * SCORE_SCALE)
            weighted = jnp.concatenate([pix[p] * prob for p in range(PIX)], axis=0)
            value_parts.append(nn(weighted.astype(bf16), ga_half))
        gv[:, at : at + LANES] = jnp.where(first, value_parts[0], value_parts[1])
        gk[:, at : at + LANES] = jnp.where(first, key_parts[0], key_parts[1])
    count = planes.shape[2]
    for b in range(planes.shape[0]):
        for p in range(PIX):
            planes[b, p] = pixg[p, b * count : (b + 1) * count, :]
    query_grad = jnp.sum(gk[...] * w[:, :D], axis=0, keepdims=True)
    for c in range(DB):
        sec32[EMBED_LINES + c : EMBED_LINES + c + 1, :] = query_grad[:, c * LANES : (c + 1) * LANES]
    grad_kv = jnp.concatenate([gk[...] * query[...], gv[...]], axis=1).astype(bf16)
    kv_grad = tn(e[...], grad_kv)
    start = EMBED_LINES + DB
    for c in range(2 * DB):
        sec32[pl.ds(start + c, D, stride=2 * DB), :] = kv_grad[:, c * LANES : (c + 1) * LANES]
    embed_grad = nt(grad_kv, kvw[...])
    for p in range(PIX):
        for c in range(DB):
            sec32[pl.ds(p * DB + c, VARS, stride=PIX * DB), :] = embed_grad[
                p * VARS : (p + 1) * VARS, c * LANES : (c + 1) * LANES
            ]
    tail = up16(HEAD_LINES) - HEAD_LINES
    sec32[HEAD_LINES:, :] = jnp.zeros((tail, LANES), f32)
    narrow_lines(sec32, up16(HEAD_LINES), sec)


def unpack_kernel(source, base, start, *refs):
    pieces = refs[: len(source.arrays)]
    qkvw, projw, upw, downw, lines = refs[len(source.arrays) :]
    source.load(pieces, base, lines)
    start = start - base
    unpack(lines, start, D, 3 * DB, qkvw)
    start += QKV_LINES
    unpack(lines, start, D, DB, projw)
    start += PROJ_LINES
    unpack(lines, start, D, FF // LANES, upw)
    start += FF_LINES
    unpack(lines, start, FF, DB, downw)


def gelu_parts(value):
    scale = math.sqrt(2.0 / math.pi)
    square = value * value
    tanh = jnp.tanh(scale * (value + 0.044715 * value * square))
    half = 0.5 * (1.0 + tanh)
    slope = half + 0.5 * value * (1.0 - tanh * tanh) * scale * (1.0 + 3.0 * 0.044715 * square)
    return value * half, slope


def pair_columns(pair):
    return [pl.ds(pl.multiple_of(pair * LANES + i * D, LANES), LANES) for i in range(3)]


def key_bias(rels, limits, rows):
    parts = []
    for rel in rels:
        position = (limits[1] ^ rel) * rows + lax.broadcasted_iota(jnp.int32, (1, rows), 1)
        parts.append(jnp.where(position < limits[0], 0.0, NEG_BIG))
    return jnp.concatenate(parts, axis=1)


def near_attend_kernel(rels, limits, *refs):
    hidden = refs[: len(rels)]
    qkvw, qkv, acc, peak, total = refs[len(rels) :]
    rows = acc.shape[0]
    for i in range(len(rels)):
        qkv[i * rows : (i + 1) * rows, :] = nn(hidden[i][...], qkvw[...]).astype(bf16)
    bias = key_bias(rels, limits, rows)
    first = lane_half((rows, LANES))
    lane = lax.broadcasted_iota(jnp.int32, (rows, LANES), 1)
    peak[...] = jnp.zeros((rows, LANES), f32)
    total[...] = jnp.zeros((rows, LANES), f32)

    def attend(pair, carry):
        at, k_at, v_at = pair_columns(pair)
        query = qkv[:rows, at] * SCORE_SCALE
        parts = []
        for half in range(2):
            scores = nt(half_of(query, half), qkv[:, k_at]) + bias
            highest = jnp.max(scores, axis=1, keepdims=True)
            exponent = jnp.exp(scores - highest)
            parts.append(nn(exponent.astype(bf16), qkv[:, v_at]))
            here = lane == pair * 2 + half
            peak[...] = jnp.where(here, highest, peak[...])
            total[...] = jnp.where(here, jnp.sum(exponent, axis=1, keepdims=True), total[...])
        acc[:, at] = jnp.where(first, parts[0], parts[1])
        return carry

    lax.fori_loop(0, HEADS // 2, attend, 0)


def layer_fwd_kernel(near, far, limits, *refs):
    hidden = refs[: len(far)]
    (qkv_near, acc, peak, near_total, res, mod, mod_next, qkvw, projw, upw, downw) = refs[
        len(far) : len(far) + 11
    ]
    (qkv, att, lse, b1, mid, pre, b2, res_next, hid_next, h_low, a_low, qkv_far) = refs[
        len(far) + 11 :
    ]
    mine = limits[1]
    rows = res.shape[0]
    for i, rel in enumerate(near):
        at = pl.multiple_of((mine ^ rel) * rows, rows)
        qkv[pl.ds(at, rows), :] = qkv_near[i * rows : (i + 1) * rows, :]
    for i, rel in enumerate(far):
        at = pl.multiple_of((mine ^ rel) * rows, rows)
        block = nn(hidden[i][...], qkvw[...]).astype(bf16)
        qkv_far[i * rows : (i + 1) * rows, :] = block
        qkv[pl.ds(at, rows), :] = block
    bias = key_bias(far, limits, rows)
    first = lane_half((rows, LANES))
    lane = lax.broadcasted_iota(jnp.int32, (rows, LANES), 1)
    lse[...] = jnp.zeros((rows, LANES), f32)

    def attend(pair, carry):
        at, k_at, v_at = pair_columns(pair)
        query = qkv_near[:rows, at] * SCORE_SCALE
        parts = []
        for half in range(2):
            here = lane == pair * 2 + half
            before = jnp.sum(jnp.where(here, peak[...], 0.0), axis=1, keepdims=True)
            total = jnp.sum(jnp.where(here, near_total[...], 0.0), axis=1, keepdims=True)
            scores = nt(half_of(query, half), qkv_far[:, k_at]) + bias
            highest = jnp.maximum(before, jnp.max(scores, axis=1, keepdims=True))
            exponent = jnp.exp(scores - highest)
            factor = jnp.exp(before - highest)
            total = total * factor + jnp.sum(exponent, axis=1, keepdims=True)
            weighted = acc[:, at] * factor + nn(exponent.astype(bf16), qkv_far[:, v_at])
            parts.append(weighted * (1.0 / total))
            lse[...] = jnp.where(here, highest + jnp.log(total), lse[...])
        att[:, at] = jnp.where(first, parts[0], parts[1])
        return carry

    lax.fori_loop(0, HEADS // 2, attend, 0)
    branch_one = nn(att[...].astype(bf16), projw[...])
    b1[...] = branch_one
    middle = res[...] + mod_row(mod, 2) * branch_one
    mid[...] = middle
    normed, unused = norm_stats(middle)
    h_low[...] = (normed * (1.0 + mod_row(mod, 4)) + mod_row(mod, 3)).astype(bf16)
    pre[...] = nn(h_low[...], upw[...])
    a_low[...] = gelu_parts(pre[...])[0].astype(bf16)
    branch_two = nn(a_low[...], downw[...])
    b2[...] = branch_two
    result = mid[...] + mod_row(mod, 5) * branch_two
    res_next[...] = result
    normed, unused = norm_stats(result)
    hid_next[...] = (normed * (1.0 + mod_row(mod_next, 1)) + mod_row(mod_next, 0)).astype(bf16)


def mlp_bwd_kernel(
    go, mod, pre, mid, b1, b2, att, lse, upw, downw, projw,
    gmid, ga_ext, delta, sums, act_low, gb2_low, h2_low, gp_low, gb1_low,
):
    rows = go.shape[0]
    grad_out = go[...]
    sums[...] = jnp.zeros(sums.shape, f32)
    put_row(sums, 5, jnp.sum(grad_out * b2[...], axis=0, keepdims=True))
    gb2_low[...] = (mod_row(mod, 5) * grad_out).astype(bf16)
    grad_act = nt(gb2_low[...], downw[...])
    act, slope = gelu_parts(pre[...])
    act_low[...] = act.astype(bf16)
    gp_low[...] = (grad_act * slope).astype(bf16)
    grad_hidden = nt(gp_low[...], upw[...])
    normed, inverse = norm_stats(mid[...])
    scale = 1.0 + mod_row(mod, 4)
    h2_low[...] = (normed * scale + mod_row(mod, 3)).astype(bf16)
    put_row(sums, 3, jnp.sum(grad_hidden, axis=0, keepdims=True))
    put_row(sums, 4, jnp.sum(grad_hidden * normed, axis=0, keepdims=True))
    grad_mid = grad_out + norm_back(grad_hidden * scale, normed, inverse)
    gmid[...] = grad_mid
    put_row(sums, 2, jnp.sum(grad_mid * b1[...], axis=0, keepdims=True))
    gb1_low[...] = (mod_row(mod, 2) * grad_mid).astype(bf16)
    grad_att = nt(gb1_low[...], projw[...]).astype(bf16)
    ga_ext[:rows, :] = grad_att
    lane = lax.broadcasted_iota(jnp.int32, (rows, LANES), 1)
    table = jnp.zeros((rows, LANES), f32)
    for h in range(HEADS):
        at = h // 2 * LANES
        prod = grad_att[:, at : at + LANES].astype(f32) * att[:, at : at + LANES]
        total = jnp.sum(half_of(prod, h % 2), axis=1, keepdims=True)
        table = jnp.where(lane == h, total, table)
    delta[...] = table
    both = jnp.where(lane < 8, lse[...], pltpu.roll(table, 8, 1))
    stats = jnp.transpose(both)[:16, :]
    high = stats.astype(bf16)
    low = (stats - high.astype(f32)).astype(bf16)
    ga_ext[rows:, :] = jnp.zeros((32, D), bf16)
    ga_ext[rows : rows + 16, :rows] = high
    ga_ext[rows + 16 : rows + 32, :rows] = low


def mlp_grads_kernel(shift, act_low, gb2_low, h2_low, gp_low, att, gb1_low, sec, sec32):
    lead = jnp.zeros((16, LANES), f32)
    sec32[0:16, :] = lead
    sec32[sec32.shape[0] - 16 :, :] = lead
    start = shift
    proj = tn(att[...].astype(bf16), gb1_low[...])
    for c in range(DB):
        sec32[pl.ds(start + c, D, stride=DB), :] = proj[:, c * LANES : (c + 1) * LANES]
    start += PROJ_LINES
    width = FF // LANES
    for c in range(0, width, 2):
        part = tn(h2_low[...], gp_low[:, c * LANES : (c + 2) * LANES])
        for k in range(2):
            sec32[pl.ds(start + c + k, D, stride=width), :] = part[
                :, k * LANES : (k + 1) * LANES
            ]
    start += FF_LINES
    for r in range(0, FF, D):
        part = tn(act_low[:, r : r + D], gb2_low[...])
        for c in range(DB):
            sec32[pl.ds(start + r * DB + c, D, stride=DB), :] = part[
                :, c * LANES : (c + 1) * LANES
            ]
    narrow_lines(sec32, sec32.shape[0], sec)


def query_bwd_kernel(limits, qkv, ga_ext, lse, delta, gq):
    length = limits[0]
    mine = limits[1]
    rows = lse.shape[0]
    seq_len = qkv.shape[0]
    position = lax.broadcasted_iota(jnp.int32, (1, seq_len), 1)
    bias = jnp.where(position < length, 0.0, NEG_BIG)
    own = pl.ds(pl.multiple_of(mine * rows, rows), rows)
    first = lane_half((rows, LANES))
    lane = lax.broadcasted_iota(jnp.int32, (rows, LANES), 1)

    def column(ref, index):
        return jnp.sum(jnp.where(lane == index, ref[...], 0.0), axis=1, keepdims=True)

    def one_pair(pair, carry):
        at, k_at, v_at = (pl.ds(pl.multiple_of(pair * LANES + i * D, LANES), LANES) for i in range(3))
        query = qkv[own, at] * SCORE_SCALE
        keys = qkv[:, k_at]
        values = qkv[:, v_at]
        grad_pair = ga_ext[:rows, at]
        parts = []
        for half in range(2):
            h = pair * 2 + half
            scores = nt(half_of(query, half), keys) + bias
            prob = jnp.exp(scores - column(lse, h))
            grad_prob = nt(half_of(grad_pair, half), values)
            grad_score = (prob * (grad_prob - column(delta, h))).astype(bf16)
            parts.append(nn(grad_score, keys) * SCORE_SCALE)
        gq[:, at] = jnp.where(first, parts[0], parts[1]).astype(bf16)
        return carry

    lax.fori_loop(0, HEADS // 2, one_pair, 0)


def keys_sums(rels, pieces, limits, qkv, stats, rows, store):
    mine = limits[1]
    own = pl.ds(pl.multiple_of(mine * rows, rows), rows)
    first = lane_half((rows, LANES))
    for i in range(len(rels)):
        both = pieces[i][rows : rows + 32, :rows].astype(f32)
        stats[i] = both[:16, :] + both[16:, :]

    def one_pair(pair, carry):
        at, k_at, v_at = (pl.ds(pl.multiple_of(pair * LANES + i * D, LANES), LANES) for i in range(3))
        keys = qkv[own, k_at] * SCORE_SCALE
        values = qkv[own, v_at]
        key_parts = []
        value_parts = []
        for half in range(2):
            h = pair * 2 + half
            key_half = half_of(keys, half)
            value_half = half_of(values, half)
            key_sum = jnp.zeros((rows, LANES), f32)
            value_sum = jnp.zeros((rows, LANES), f32)
            for i, rel in enumerate(rels):
                there = pl.ds(pl.multiple_of((mine ^ rel) * rows, rows), rows)
                query = qkv[there, at]
                grad_pair = pieces[i][:rows, at]
                prob = jnp.exp(nt(key_half, query) - stats[i, pl.ds(h, 1), :])
                grad_prob = nt(value_half, grad_pair)
                grad_score = (prob * (grad_prob - stats[i, pl.ds(8 + h, 1), :])).astype(bf16)
                key_sum += nn(grad_score, query)
                value_sum += nn(prob.astype(bf16), grad_pair)
            key_parts.append(key_sum * SCORE_SCALE)
            value_parts.append(value_sum)
        store(
            at,
            jnp.where(first, key_parts[0], key_parts[1]),
            jnp.where(first, value_parts[0], value_parts[1]),
        )
        return carry

    lax.fori_loop(0, HEADS // 2, one_pair, 0)


def near_keys_kernel(rels, limits, *refs):
    pieces = refs[: len(rels)]
    qkv, key_out, value_out, stats = refs[len(rels) :]

    def store(at, key_sum, value_sum):
        key_out[:, at] = key_sum
        value_out[:, at] = value_sum

    keys_sums(rels, pieces, limits, qkv, stats, key_out.shape[0], store)


def keys_bwd_kernel(rels, limits, *refs):
    pieces = refs[: len(rels)]
    (qkv, gq, key_near, value_near, res, mod, qkvw, gmid) = refs[len(rels) : len(rels) + 8]
    (gqkv, go_prev, sums, stats) = refs[len(rels) + 8 :]
    rows = res.shape[0]
    position = limits[1] * rows + lax.broadcasted_iota(jnp.int32, (rows, 1), 0)
    live = position < limits[0]
    gqkv[:, :D] = gq[...]

    def store(at, key_sum, value_sum):
        k_at, v_at = (pl.ds(pl.multiple_of(at.start + i * D, LANES), LANES) for i in (1, 2))
        gqkv[:, k_at] = jnp.where(live, key_near[:, at] + key_sum, 0.0).astype(bf16)
        gqkv[:, v_at] = jnp.where(live, value_near[:, at] + value_sum, 0.0).astype(bf16)

    keys_sums(rels, pieces, limits, qkv, stats, rows, store)
    grad_hidden = nt(gqkv[...], qkvw[...])
    normed, inverse = norm_stats(res[...])
    sums[...] = jnp.zeros(sums.shape, f32)
    put_row(sums, 0, jnp.sum(grad_hidden, axis=0, keepdims=True))
    put_row(sums, 1, jnp.sum(grad_hidden * normed, axis=0, keepdims=True))
    scale = 1.0 + mod_row(mod, 1)
    go_prev[...] = gmid[...] + norm_back(grad_hidden * scale, normed, inverse)


def qkv_grads_kernel(shift, hidden, gqkv, sec, sec32):
    sec32[0:16, :] = jnp.zeros((16, LANES), f32)
    sec32[sec32.shape[0] - 16 :, :] = jnp.zeros((16, LANES), f32)
    width = 3 * DB
    for c in range(0, width, DB):
        part = tn(hidden[...], gqkv[:, c * LANES : (c + DB) * LANES])
        for k in range(DB):
            sec32[pl.ds(shift + c + k, D, stride=width), :] = part[:, k * LANES : (k + 1) * LANES]
    narrow_lines(sec32, sec32.shape[0], sec)


def axis_dims(axis, count):
    dims = []
    for bit in range((count - 1).bit_length()):
        dims.append((axis, [i ^ (1 << bit) for i in range(count)], [i >> bit & 1 for i in range(count)]))
    return dims


def together(values):
    return lax.optimization_barrier(values)


def total_of(parts, begin, end):
    return sum(part[begin:end].astype(f32) for part in parts)


class Cube:
    def __init__(self, var_count, dp_count):
        self.dp_count = dp_count
        self.owners = var_count * dp_count
        var_dims = axis_dims("var", var_count)
        self.core = var_dims[0]
        self.dims = var_dims[1:] + axis_dims("dp", dp_count)

    def partner(self, owner, dim):
        axis, partner, unused = dim
        v, d = divmod(owner, self.dp_count)
        if axis == "var":
            return partner[v] * self.dp_count + d
        return v * self.dp_count + partner[d]

    def bit(self, owner, dim):
        axis, unused, bits = dim
        v, d = divmod(owner, self.dp_count)
        return bits[v] if axis == "var" else bits[d]

    def hop(self, value, *dims, core=None):
        pairs = []
        for owner in range(self.owners):
            other = owner
            for dim in dims:
                other = self.partner(other, dim)
            if core is None or self.bit(owner, self.core) == core:
                pairs.append((owner, other))
        return self.send(value, pairs)

    def send(self, value, pairs):
        return lax.ppermute(value, ("var", "dp"), pairs)

    def mine(self):
        return lax.axis_index("var") * self.dp_count + lax.axis_index("dp")

    def exchange_sum(self, value, groups):
        for group in groups:
            terms = [value]
            for mask in range(1, 2 ** len(group)):
                terms.append(self.hop(value, *[d for i, d in enumerate(group) if mask >> i & 1]))
            while len(terms) > 1:
                terms = [terms[i] + terms[i + 1] for i in range(0, len(terms), 2)]
            value = terms[0]
        return value


PLAN_SHAPE = (4, 8, 1440)
HALF = 720
NEEDED_ZERO = {0: 3, 1: 3, 2: 3, 3: 1, 7: 2, 16: 3, 17: 3, 22: 3, 23: 3}
ENTRIES = (
    [(o, h) for o in (0, 1, 2) for h in (0, 1)]
    + [(3, 0), (7, 1)]
    + [(o, h) for o in range(8, 18) for h in (0, 1)]
    + [(o, h) for o in range(22, 32) for h in (0, 1)]
)


class Plan:
    def __init__(self, cube):
        self.cube = cube
        x, y, step, pair = cube.dims
        self.pair = pair
        self.orders = ((y, x, step), (step, y, x), (step, x, y))
        self.back_orders = ((y, x, step), (x, step, y), (step, y, x))
        back = [order[::-1] for order in self.back_orders]
        rows = [
            self.codes(o, self.orders) + self.codes(o, back) + self.flags(o)
            for o in range(cube.owners)
        ]
        row = jnp.asarray(rows, jnp.int32)[cube.mine()]
        self.table = row[: len(ENTRIES)]
        self.back_table = row[len(ENTRIES) : 2 * len(ENTRIES)]
        self.flag = [row[2 * len(ENTRIES) + i] == 1 for i in range(3)]
        ones = [o for o in range(cube.owners) if cube.bit(o, cube.core)]
        self.ones_pairs = [(o, cube.partner(o, pair)) for o in ones]
        self.zero_pairs = [(o, cube.partner(o, pair)) for o in NEEDED_ZERO]

    def flags(self, device):
        needed = NEEDED_ZERO.get(device, 0)
        return [self.cube.bit(device, self.cube.core), needed & 1, needed >> 1]

    def codes(self, device, orders):
        cube = self.cube
        codes = []
        for owner, half in ENTRIES:
            chunk = 1 + half
            stream = cube.bit(owner, cube.core)
            if stream == 1 and cube.bit(owner, self.pair) == cube.bit(device, self.pair):
                chunk = 0
                stream = 1 - half
            place = 0
            for s, dim in enumerate(orders[chunk]):
                place += (cube.bit(owner, dim) ^ cube.bit(device, dim)) << s
            codes.append(chunk * 16 + (stream ^ cube.bit(device, cube.core)) * 8 + place)
        return codes

    def gather(self, shard, early, sums, first_work, second_work):
        cube = self.cube
        is_one, own_first, own_second = self.flag

        def hop(chunk, step):
            return cube.hop(current[chunk], self.orders[chunk][step])

        def grow(chunk, got):
            current[chunk] = jnp.concatenate([current[chunk], got], axis=0)

        lower = cube.hop(shard[HALF:], cube.core)
        from_one = cube.send(shard, self.ones_pairs)
        from_zero = cube.send(shard, self.zero_pairs)
        current = [jnp.where(is_one, shard[:HALF], lower)[None], None, None]
        grow(0, hop(0, 0))
        from_one, from_zero, current[0], early, sums = together(
            (from_one, from_zero, current[0], early, sums)
        )
        first = jnp.where(own_first, shard[:HALF], from_zero[:HALF])
        second = jnp.where(own_second, shard[HALF:], from_zero[HALF:])
        current[1] = jnp.where(is_one, from_one[:HALF], first)[None]
        current[2] = jnp.where(is_one, from_one[HALF:], second)[None]
        sums = first_work(sums)
        got = [hop(0, 1), hop(1, 0), hop(2, 0)]
        for chunk in range(3):
            grow(chunk, got[chunk])
        current, sums = together((current, sums))
        done = second_work(sums)
        last = [hop(0, 2), None, None]
        got = [hop(1, 1), hop(2, 1)]
        for chunk in range(2):
            grow(chunk + 1, got[chunk])
        current[1], current[2], done = together((current[1], current[2], done))
        last[1], last[2] = hop(1, 2), hop(2, 2)
        other = [cube.hop(value, cube.core) for value in current]
        other_last = [cube.hop(value, cube.core) for value in last]
        pieces = [entry for group in zip(current, last, other, other_last) for entry in group]
        return pieces, early, done

    def scatter(self, keep, send, late, work):
        cube = self.cube
        is_one, own_first, own_second = self.flag
        parts = [[a, cube.hop(b, cube.core)] for a, b in zip(keep, send)]
        half = 4
        for step in range(3):
            outs = [total_of(part, half, 2 * half).astype(bf16) for part in parts]
            for q in range(3):
                got = cube.hop(outs[q], self.back_orders[q][step])
                parts[q] = [part[:half] for part in parts[q]] + [got]
            half //= 2
        first, second, third = (total_of(part, 0, 1)[0] for part in parts)
        back = [(b, a) for a, b in self.ones_pairs + self.zero_pairs]
        low = [second.astype(bf16), third.astype(bf16), first.astype(bf16)]
        low[1], low[2] = together((low[1], low[2]))
        partner = [cube.send(part, back).astype(f32) for part in low[:2]]
        lower, late = together((cube.hop(low[2], cube.core), late))
        lower = lower.astype(f32)
        partner[1], late = together((partner[1], work(late)))
        halves = [
            jnp.where(is_one, first, second) + partner[0],
            jnp.where(is_one, lower, third) + partner[1],
        ]
        return jnp.concatenate(halves, axis=0), late


def flip(value, axis, bit):
    count = lax.axis_size(axis)
    return lax.ppermute(value, axis, [(i, i ^ bit) for i in range(count)])


NEAR = (0, 1)


def gather_blocks(value, work):
    count = lax.axis_size("var")
    pieces = {0: value, 1: flip(value, "var", 1)}
    done = work([pieces[r] for r in NEAR])
    bit = count // 2
    while bit > 1:
        got = {r ^ bit: flip(piece, "var", bit) for r, piece in pieces.items() if r % 2 == 0}
        if bit == 2:
            got, done = together((got, done))
        pieces.update(got)
        bit //= 2
    for r in range(2, count, 2):
        pieces[r + 1] = flip(pieces[r], "var", 1)
    return [pieces[r] for r in range(count)], done


def local(pixels, var_mask, lengths, condition, cotangent, master, moment_one, moment_two):
    var_count = lax.axis_size("var")
    dp_count = lax.axis_size("dp")
    var_index = lax.axis_index("var")
    rows = cotangent.shape[1]
    seq_len = rows * var_count
    local_vars = pixels.shape[0]
    shard_lines = master.shape[0] // LANES
    total_lines = shard_lines * var_count * dp_count

    shard = master.astype(bf16).reshape(shard_lines, LANES)
    present = jnp.where(var_mask == 1, 1.0, 0.0).astype(bf16)
    planes = jnp.concatenate(
        [pixels[:, :, 0, :], jnp.broadcast_to(present[:, None, None], (local_vars, 1, seq_len))],
        axis=1,
    )
    planes = planes.reshape(local_vars, PIX + 1, var_count, rows).transpose(2, 1, 0, 3)

    def spread(values):
        return lax.all_to_all(values, "var", 0, 0, tiled=True)

    cube = Cube(var_count, dp_count)
    planned = (var_count, dp_count, shard_lines) == PLAN_SHAPE
    cond_low = jax.nn.silu(condition.astype(f32)).astype(bf16)
    limits = jnp.stack([lengths[0], var_index.astype(jnp.int32)])
    if planned:
        plan = Plan(cube)
        dp_index = lax.axis_index("dp")
        slots = LAYERS * BIAS_LINES
        x = cube.dims[0]

        def to_all(value):
            copies = jnp.broadcast_to(value[None], (dp_count,) + value.shape)
            return lax.all_to_all(copies, "dp", 0, 0, tiled=True)

        conds = to_all(cond_low[0].reshape(DB, LANES)).reshape(dp_count, D)
        of_slot = jnp.arange(dp_count * slots) // slots
        ada_table, partial = run(
            functools.partial(ada_kernel, shard_lines),
            "ada",
            [shape((shard_lines, dp_count * slots), bf16), shape((dp_count * slots, LANES), f32)],
            [
                cube.mine()[None].astype(jnp.int32), shard, conds,
                (jnp.arange(dp_count)[:, None] == of_slot[None, :]).astype(bf16),
                (jnp.arange(dp_count * slots) % slots)[None, :].astype(jnp.int32),
            ],
            [SM] + [VM] * 4,
            [pltpu.VMEM((shard_lines, D), bf16)],
            flops=10**9,
        )
        def first_work(sums):
            sums = sums.reshape(dp_count, slots, LANES)
            return jnp.sum(lax.all_to_all(sums, "dp", 0, 0, tiled=True), axis=0)

        def second_work(sums):
            return cube.exchange_sum(sums, [[cube.core], [x]])

        pieces, planes, own = plan.gather(shard, spread(planes), partial, first_work, second_work)
        arrays = [plan.table, *pieces]
        specs = [SM] + [VM] * len(pieces)
        mods = [own[layer * BIAS_LINES : (layer + 1) * BIAS_LINES] for layer in range(LAYERS)]
    else:
        planes = spread(planes)
        arrays = [lax.all_gather(shard, ("var", "dp"), axis=0, tiled=True)]
        specs = [VM]
        mods = []
        for layer in range(LAYERS):
            start = HEAD_LINES + layer * LAYER_LINES
            ada = arrays[0][start : start + ADA_LINES].reshape(D, 6 * D)
            bias = arrays[0][start + ADA_LINES : start + ADA_LINES + BIAS_LINES]
            mods.append(
                jnp.dot(cond_low, ada, preferred_element_type=f32).reshape(BIAS_LINES, LANES)
                + bias.astype(f32)
            )
    mods = [jnp.pad(mod, ((0, 24 - BIAS_LINES), (0, 0))) for mod in mods]
    source = Source(arrays, specs, planned)

    begin, end = source.span(0, HEAD_LINES)
    (residual, hidden, agg_low, probs, w, u, e, kvw, aggw, query, pix) = run(
        functools.partial(agg_fwd_kernel, source),
        "agg_fwd",
        [
            shape((rows, D), f32), shape((rows, D), bf16), shape((rows, D), bf16),
            shape((HEADS, VARS, rows), f32), shape((VP, 2 * D), f32), shape((VP, LANES), f32),
            shape((VP, D), bf16), shape((D, 2 * D), bf16), shape((D, D), bf16),
            shape((1, D), f32), shape((PIX, VARS, rows), f32),
        ],
        [*arrays, planes, mods[0]],
        [*specs, VM, VM],
        [
            pltpu.VMEM((end - begin, LANES), f32), pltpu.VMEM((VP, D), f32),
            pltpu.VMEM((VARS, LANES), f32),
        ],
        flops=10**9,
    )

    def unpack_layer(layer):
        start = HEAD_LINES + layer * LAYER_LINES + ADA_LINES + BIAS_LINES
        begin, end = source.span(start, HEAD_LINES + (layer + 1) * LAYER_LINES)
        return run(
            functools.partial(unpack_kernel, source, begin, start),
            f"unpack_{layer}",
            [
                shape((D, 3 * D), bf16), shape((D, D), bf16), shape((D, FF), bf16),
                shape((FF, D), bf16),
            ],
            arrays,
            specs,
            [pltpu.VMEM((end - begin, LANES), f32)],
            flops=10**9,
        )

    weights = [None] * LAYERS

    def begin_layer(layer, value):
        def work(blocks):
            weights = unpack_layer(layer)
            return weights, run(
                functools.partial(near_attend_kernel, NEAR),
                f"near_attend_{layer}",
                [
                    shape((len(NEAR) * rows, 3 * D), bf16), shape((rows, D), f32),
                    shape((rows, LANES), f32), shape((rows, LANES), f32),
                ],
                [limits, *blocks, weights[0]],
                [SM] + [VM] * (len(NEAR) + 1),
                flops=10**9,
            )

        blocks, (weights[layer], attention) = gather_blocks(value, work)
        return blocks, attention

    hidden_blocks, partial_attention = begin_layer(0, hidden)

    stored = []
    for layer in range(LAYERS):
        qkvw, projw, upw, downw = weights[layer]
        mod = mods[layer]
        mod_next = mods[min(layer + 1, LAYERS - 1)]
        blocks = hidden_blocks
        outs = [
            shape((seq_len, 3 * D), bf16), shape((rows, D), f32), shape((rows, LANES), f32),
            shape((rows, D), f32), shape((rows, D), f32), shape((rows, FF), f32),
            shape((rows, D), f32), shape((rows, D), f32), shape((rows, D), bf16),
        ]
        near, far = NEAR, tuple(range(len(NEAR), var_count))
        qkv, att, lse, b1, mid, pre, b2, next_residual, next_hidden = run(
            functools.partial(layer_fwd_kernel, near, far),
            f"layer_fwd_{layer}",
            outs,
            [
                limits, *(blocks[r] for r in far), *partial_attention, residual, mod, mod_next,
                qkvw, projw, upw, downw,
            ],
            [SM] + [VM] * (len(far) + 11),
            [
                pltpu.VMEM((rows, D), bf16), pltpu.VMEM((rows, FF), bf16),
                pltpu.VMEM((len(far) * rows, 3 * D), bf16),
            ],
            flops=4 * 10**9,
        )
        stored.append((hidden, residual, qkv, att, lse, b1, mid, pre, b2))
        residual, hidden = next_residual, next_hidden
        if layer + 1 < LAYERS:
            hidden_blocks, partial_attention = begin_layer(layer + 1, hidden)
    output = residual

    grad_out = cotangent[0]
    sections = []
    ada_sums = [None] * LAYERS
    for layer in reversed(range(LAYERS)):
        qkvw, projw, upw, downw = weights[layer]
        mod = mods[layer]
        hidden, residual, qkv, att, lse, b1, mid, pre, b2 = stored[layer]
        first_line = HEAD_LINES + layer * LAYER_LINES
        outs = [
            shape((rows, D), f32), shape((rows + 32, D), bf16), shape((rows, LANES), f32),
            shape((24, LANES), f32), shape((rows, FF), bf16), shape((rows, D), bf16),
            shape((rows, D), bf16), shape((rows, FF), bf16), shape((rows, D), bf16),
        ]
        gmid, ga_ext, delta, sums_a, act_low, gb2_low, h2_low, gp_low, gb1_low = run(
            mlp_bwd_kernel,
            f"mlp_bwd_{layer}",
            outs,
            [grad_out, mod, pre, mid, b1, b2, att, lse, upw, downw, projw],
            flops=2 * 10**9,
        )

        def work(near_blocks, layer=layer, qkv=qkv, ga_ext=ga_ext, lse=lse, delta=delta):
            (gq,) = run(
                query_bwd_kernel,
                f"query_bwd_{layer}",
                [shape((rows, D), bf16)],
                [limits, qkv, ga_ext, lse, delta],
                [SM] + [VM] * 4,
                flops=4 * 10**9,
            )
            return gq, run(
                functools.partial(near_keys_kernel, NEAR),
                f"near_keys_{layer}",
                [shape((rows, D), f32), shape((rows, D), f32)],
                [limits, *near_blocks, qkv],
                [SM] + [VM] * (len(NEAR) + 1),
                [pltpu.VMEM((len(NEAR), 16, rows), f32)],
                flops=3 * 10**9,
            )

        blocks, (gq, (key_near, value_near)) = gather_blocks(ga_ext, work)
        start = first_line + ADA_LINES + BIAS_LINES + QKV_LINES
        count = up16(start + PROJ_LINES + 2 * FF_LINES) - down16(start)
        (section,) = run(
            functools.partial(mlp_grads_kernel, start - down16(start)),
            f"mlp_grads_{layer}",
            [shape((count, LANES), bf16)],
            [act_low, gb2_low, h2_low, gp_low, att, gb1_low],
            scratch=[pltpu.VMEM((count, LANES), f32)],
            flops=2 * 10**9,
        )
        sections.append((start, PROJ_LINES + 2 * FF_LINES, section))
        far = tuple(range(len(NEAR), var_count))
        gqkv, grad_out, sums_b = run(
            functools.partial(keys_bwd_kernel, far),
            f"keys_bwd_{layer}",
            [shape((rows, 3 * D), bf16), shape((rows, D), f32), shape((24, LANES), f32)],
            [
                limits, *(blocks[r] for r in far), qkv, gq, key_near, value_near, residual, mod, qkvw,
                gmid,
            ],
            [SM] + [VM] * (len(far) + 8),
            [pltpu.VMEM((len(far), 16, rows), f32)],
            flops=3 * 10**9,
        )
        start = first_line + ADA_LINES + BIAS_LINES
        count = up16(start + QKV_LINES) - down16(start)
        (section,) = run(
            functools.partial(qkv_grads_kernel, start - down16(start)),
            f"qkv_grads_{layer}",
            [shape((count, LANES), bf16)],
            [hidden, gqkv],
            scratch=[pltpu.VMEM((count, LANES), f32)],
            flops=10**9,
        )
        sections.append((start, QKV_LINES, section))
        ada_sums[layer] = (sums_a + sums_b)[:BIAS_LINES]

    pixel_grad, section = run(
        agg_bwd_kernel,
        "agg_bwd",
        [
            shape((var_count, PIX, local_vars, rows), f32),
            shape((up16(HEAD_LINES), LANES), bf16),
        ],
        [grad_out, agg_low, probs, w, u, e, kvw, aggw, query, pix],
        scratch=[
            pltpu.VMEM((up16(HEAD_LINES), LANES), f32), pltpu.VMEM((VP, D), f32),
            pltpu.VMEM((VP, D), f32), pltpu.VMEM((PIX, VARS, rows), f32),
        ],
        flops=10**9,
    )
    sections.append((0, HEAD_LINES, section))
    def unspread(values):
        return lax.all_to_all(values, "var", 0, 0, tiled=True)

    if planned:
        sections.sort(key=lambda entry: entry[0])
        meta = [(down16(start), part.shape[0]) for start, count, part in sections]
        own = cube.exchange_sum(jnp.concatenate(ada_sums, axis=0), [[cube.core], [x]])
        parts, own = together(([s[2] for s in sections], own))
        packed = run(
            functools.partial(pack_kernel, meta),
            "pack",
            [shape((8, HALF, LANES), bf16)] * 6,
            [
                plan.back_table,
                *parts,
            ],
            [SM] + [VM] * len(sections),
            [pltpu.VMEM((len(ENTRIES) * HALF, LANES), bf16)],
        )

        def beside_scatter(values):
            own, grads = values
            return to_all(own), unspread(grads)

        grad_lines, (sums, pixel_grad) = plan.scatter(
            packed[::2], packed[1::2], (own, pixel_grad), beside_scatter
        )
        sums = sums.reshape(dp_count * slots, LANES)
        high = sums.astype(bf16)
        low = (sums - high.astype(f32)).astype(bf16)
        ada_lines = nn(ada_table, high) + nn(ada_table, low)
        line = cube.mine() * shard_lines + lax.broadcasted_iota(jnp.int32, (shard_lines, 1), 0)
        for layer in range(LAYERS):
            start = HEAD_LINES + layer * LAYER_LINES
            inside = jnp.logical_and(line >= start, line < start + ADA_LINES + BIAS_LINES)
            grad_lines = jnp.where(inside, ada_lines, grad_lines)
    else:
        pixel_grad = unspread(pixel_grad)
        for layer in range(LAYERS):
            start = HEAD_LINES + layer * LAYER_LINES
            outer = cond_low[0].astype(f32)[:, None, None] * ada_sums[layer][None]
            outer = outer.reshape(ADA_LINES, LANES).astype(bf16)
            shift = start - down16(start)
            outer = jnp.concatenate(
                [jnp.zeros((shift, LANES), bf16), outer, ada_sums[layer].astype(bf16)], axis=0
            )
            sections.append((start, ADA_LINES + BIAS_LINES, outer))
        sections.sort(key=lambda entry: entry[0])
        parts = [
            part[start - down16(start) : start - down16(start) + count]
            for start, count, part in sections
        ]
        used = sections[-1][0] + sections[-1][1]
        parts.append(jnp.zeros((total_lines - used, LANES), bf16))
        whole = jnp.concatenate(parts, axis=0)
        grad_lines = lax.psum_scatter(
            whole, ("var", "dp"), scatter_dimension=0, tiled=True
        ).astype(f32)
    patch_grads = pixel_grad.transpose(2, 1, 0, 3).reshape(local_vars, PIX, seq_len)
    grad_shard = grad_lines.reshape(-1)
    squares = jnp.sum(grad_shard * grad_shard)
    if planned:
        copies = jnp.broadcast_to(squares, (cube.owners, 1, LANES))
        copies = lax.all_to_all(copies, ("var", "dp"), 0, 0, tiled=True)
        squares = jnp.sum(copies, axis=0)[0, 0]
    else:
        squares = lax.psum(squares, ("var", "dp"))
    grad_norm = jnp.sqrt(squares)
    clip_limit = CLIP_COEF * math.sqrt(PARAMS * seq_len * dp_count)
    clipped = grad_shard * (clip_limit / jnp.maximum(grad_norm, clip_limit))
    new_one = BETA_ONE * moment_one + (1.0 - BETA_ONE) * clipped
    new_two = BETA_TWO * moment_two + (1.0 - BETA_TWO) * clipped * clipped
    ratio = (
        new_one / (1.0 - BETA_ONE**STEP) / (jnp.sqrt(new_two / (1.0 - BETA_TWO**STEP)) + ADAM_EPS)
    )
    new_master = master - LEARN_RATE * (ratio + WEIGHT_DECAY * master)
    return (
        output[None],
        patch_grads[:, :, None, :],
        grad_norm,
        new_master,
        new_one,
        new_two,
        new_master.astype(bf16),
    )


def solution(mesh):
    in_specs = (
        P("var", None, "dp", None),
        P("var"),
        P("dp"),
        P("dp", None),
        P("dp", "var", None),
        P(("var", "dp")),
        P(("var", "dp")),
        P(("var", "dp")),
    )
    out_specs = (
        P("dp", "var", None),
        P("var", None, "dp", None),
        P(),
        P(("var", "dp")),
        P(("var", "dp")),
        P(("var", "dp")),
        P(("var", "dp")),
    )
    return jax.shard_map(local, mesh=mesh, in_specs=in_specs, out_specs=out_specs, check_vma=False)
```

```python
import functools
import math

import jax
import jax.numpy as jnp
from jax import lax
from jax.experimental import pallas as pl
from jax.experimental.pallas import tpu as pltpu
from jax.sharding import PartitionSpec as P

D = 384
HEADS = 6
HEAD_DIM = D // HEADS
FF = 1536
VARS = 72
PIX = 4
LAYERS = 2
STEP = 3
PARAMS = 5866368

NEG_BIG = -1e30
NORM_EPS = 1e-06
CLIP_COEF = 0.005
LEARN_RATE = 0.06
WEIGHT_DECAY = 0.1
ADAM_EPS = 1e-08
BETA_ONE = 0.5
BETA_TWO = 0.5
SCORE_SCALE = HEAD_DIM ** (-0.5)

LANES = 128
DB = D // LANES
VP = VARS * PIX
ADA_LINES = 6 * D * D // LANES
BIAS_LINES = 6 * DB
QKV_LINES = 3 * D * D // LANES
PROJ_LINES = D * D // LANES
FF_LINES = D * FF // LANES
EMBED_LINES = VP * DB
KV_LINES = 2 * D * D // LANES
HEAD_LINES = EMBED_LINES + DB + KV_LINES + PROJ_LINES
LAYER_LINES = ADA_LINES + BIAS_LINES + QKV_LINES + PROJ_LINES + 2 * FF_LINES

bf16 = jnp.bfloat16
f32 = jnp.float32


def down16(value):
    return value // 16 * 16


def up16(value):
    return (value + 15) // 16 * 16


def nn(left, right):
    return lax.dot_general(left, right, (((1,), (0,)), ((), ())), preferred_element_type=f32)


def nt(left, right):
    return lax.dot_general(left, right, (((1,), (1,)), ((), ())), preferred_element_type=f32)


def tn(left, right):
    return lax.dot_general(left, right, (((0,), (0,)), ((), ())), preferred_element_type=f32)


def nn_f32(left, right, dims):
    return lax.dot_general(
        left,
        right,
        (dims, ((), ())),
        preferred_element_type=f32,
        precision=lax.Precision.HIGHEST,
    )


VMEM_MIB = {
    "ada": 14,
    "agg_fwd": 14,
    "unpack": 14,
    "near_attend": 16,
    "layer_fwd": 24,
    "mlp_bwd": 16,
    "query_bwd": 16,
    "mlp_grads": 12,
    "near_keys": 16,
    "keys_bwd": 16,
    "qkv_grads": 10,
    "agg_bwd": 14,
    "pack": 16,
}

VM = pl.BlockSpec(memory_space=pltpu.VMEM)
SM = pl.BlockSpec(memory_space=pltpu.SMEM)
ANY = pl.BlockSpec(memory_space=pl.ANY)


def run(kernel, name, outs, ins, in_specs=None, scratch=(), flops=0, out_specs=None):
    if in_specs is None:
        in_specs = [VM] * len(ins)
    nbytes = sum(math.prod(o.shape) * o.dtype.itemsize for o in outs)
    nbytes += sum(math.prod(i.shape) * i.dtype.itemsize for i in ins)
    return pl.pallas_call(
        kernel,
        name=name,
        out_shape=outs,
        in_specs=in_specs,
        out_specs=out_specs or [VM] * len(outs),
        scratch_shapes=list(scratch),
        cost_estimate=pl.CostEstimate(flops=flops, bytes_accessed=nbytes, transcendentals=0),
        compiler_params=pltpu.CompilerParams(vmem_limit_bytes=VMEM_MIB[name.rstrip("_0123456789")] * 2**20),
    )(*ins)


def shape(dims, dtype):
    return jax.ShapeDtypeStruct(dims, dtype)


def mod_row(ref, index):
    return jnp.concatenate(
        [ref[DB * index + c : DB * index + c + 1, :] for c in range(DB)], axis=1
    )


def norm_stats(values):
    centered = values - jnp.mean(values, axis=-1, keepdims=True)
    inverse = lax.rsqrt(jnp.mean(centered * centered, axis=-1, keepdims=True) + NORM_EPS)
    return centered * inverse, inverse


def norm_back(grad_normed, normed, inverse):
    mean_grad = jnp.mean(grad_normed, axis=-1, keepdims=True)
    mean_cross = jnp.mean(grad_normed * normed, axis=-1, keepdims=True)
    return inverse * (grad_normed - mean_grad - normed * mean_cross)


def lane_half(shape_):
    return lax.broadcasted_iota(jnp.int32, shape_, 1) < HEAD_DIM


def half_of(pair, half):
    first = lane_half(pair.shape)
    keep = first if half == 0 else jnp.logical_not(first)
    return jnp.where(keep, pair, jnp.zeros_like(pair))


def put_row(ref, index, row):
    for c in range(DB):
        ref[DB * index + c : DB * index + c + 1, :] = row[:, c * LANES : (c + 1) * LANES]


def narrow_lines(src, count, dst):
    step = 512
    whole = count // step

    def body(i, carry):
        row = pl.multiple_of(i * step, step)
        dst[pl.ds(row, step), :] = src[pl.ds(row, step), :].astype(bf16)
        return carry

    if whole:
        lax.fori_loop(0, whole, body, 0)
    rest = count - whole * step
    if rest:
        dst[whole * step : count, :] = src[whole * step : count, :].astype(bf16)


def unpack(lines, start, rows, blocks, out):
    for c in range(blocks):
        out[:, c * LANES : (c + 1) * LANES] = lines[
            pl.ds(start + c, rows, stride=blocks), :
        ].astype(bf16)


class Source:
    def __init__(self, arrays, specs, planned):
        self.arrays = arrays
        self.specs = specs
        self.planned = planned

    def span(self, start, end):
        if not self.planned:
            return down16(start), up16(end)
        return start // HALF * HALF, -(-end // HALF) * HALF

    def load(self, refs, base, lines):
        if not self.planned:
            lines[...] = refs[0][base : base + lines.shape[0], :].astype(f32)
            return
        table = refs[0]
        starts = [o * 2 * HALF + h * HALF for o, h in ENTRIES]
        first = starts.index(base)
        count = lines.shape[0] // HALF
        assert starts[first : first + count] == [base + i * HALF for i in range(count)]

        def body(index, carry):
            code = table[first + index]
            place = code % 4
            at = pl.multiple_of(index * HALF, 16)
            for k in range(12):

                @pl.when(code // 4 == k)
                def copy_block(k=k):
                    lines[pl.ds(at, HALF), :] = refs[1 + k][place].astype(f32)

            return carry

        lax.fori_loop(0, count, body, 0)


def ada_kernel(shard_lines, place, shard, cond_all, spread, column, table, partial, hot):
    line = place[0] * shard_lines + lax.broadcasted_iota(jnp.int32, (shard_lines, 1), 0)
    feature = lax.broadcasted_iota(jnp.int32, (1, D), 1)
    target = jnp.full((shard_lines, 1), -1, jnp.int32)
    is_bias = jnp.zeros((shard_lines, 1), jnp.int32)
    rank = jnp.full((shard_lines, 1), -1, jnp.int32)
    for layer in range(LAYERS):
        begin = HEAD_LINES + layer * LAYER_LINES
        here = jnp.logical_and(line >= begin, line < begin + ADA_LINES)
        rank = jnp.where(here, line - begin, rank)
        target = jnp.where(here, layer * BIAS_LINES, target)
        bias = jnp.logical_and(
            line >= begin + ADA_LINES, line < begin + ADA_LINES + BIAS_LINES
        )
        target = jnp.where(bias, layer * BIAS_LINES + line - begin - ADA_LINES, target)
        is_bias = jnp.where(bias, 1, is_bias)
    passed = rank >= (feature + 1) * BIAS_LINES
    row = jnp.sum(passed.astype(f32), axis=1, keepdims=True).astype(jnp.int32)
    hot[...] = jnp.where(
        jnp.logical_and(rank >= 0, row == feature), 1.0, 0.0
    ).astype(bf16)
    target = jnp.where(rank >= 0, target + rank - row * BIAS_LINES, target)
    factors = nt(hot[...], cond_all[...])
    factors = nn(factors.astype(bf16), spread[...])
    factors = jnp.where(is_bias > 0, 1.0, factors)
    table[...] = jnp.where(target == column[...], factors, 0.0).astype(bf16)
    partial[...] = tn(table[...], shard[...])


def copy_lines(src, start, count, dst, at):
    step = 512
    whole = count // step

    def body(i, carry):
        row = pl.multiple_of(i * step, step)
        dst[pl.ds(at + row, step), :] = src[pl.ds(start + row, step), :]
        return carry

    if whole:
        lax.fori_loop(0, whole, body, 0)
    rest = count - whole * step
    if rest:
        dst[at + whole * step : at + count, :] = src[start + whole * step : start + count, :]


def pack_kernel(meta, table, *refs):
    sections = refs[: len(meta)]
    targets = refs[len(meta) : len(meta) + 6]
    lines = refs[len(meta) + 6]
    starts = [o * 2 * HALF + h * HALF for o, h in ENTRIES]
    end = 0
    tile = None
    for i, (base, size) in enumerate(meta):
        entry = max(e for e, start in enumerate(starts) if start <= base)
        base = base - starts[entry] + entry * HALF
        if base > end:
            lines[end:base, :] = jnp.zeros((base - end, LANES), bf16)
        copy_lines(sections[i], 0, size, lines, base)
        if base < end:
            lines[base:end, :] = lines[base:end, :] + tile
        tile = sections[i][size - 16 : size, :]
        end = base + size
    lines[end:, :] = jnp.zeros((lines.shape[0] - end, LANES), bf16)

    def body(index, carry):
        code = table[index]
        at = pl.multiple_of(index * HALF, 16)
        for k, target in enumerate(targets):

            @pl.when(code // 8 == k)
            def copy_block(target=target):
                target[code % 8] = lines[pl.ds(at, HALF), :]

        return carry

    lax.fori_loop(0, len(ENTRIES), body, 0)


def agg_fwd_kernel(source, *refs):
    pieces = refs[: len(source.arrays)]
    (
        planes, mod,
        res, hid, agg_low, probs, w, u, e, kvw, aggw, query, pix,
        lines, e32, mask,
    ) = refs[len(source.arrays) :]
    source.load(pieces, 0, lines)
    for p in range(PIX):
        for c in range(DB):
            e32[p * VARS : (p + 1) * VARS, c * LANES : (c + 1) * LANES] = lines[
                pl.ds(p * DB + c, VARS, stride=PIX * DB), :
            ]
    e[...] = e32[...].astype(bf16)
    query[...] = jnp.concatenate(
        [lines[EMBED_LINES + c : EMBED_LINES + c + 1, :] for c in range(DB)], axis=1
    )
    unpack(lines, EMBED_LINES + DB, D, 2 * DB, kvw)
    unpack(lines, EMBED_LINES + DB + KV_LINES, D, DB, aggw)
    w[...] = nn(e[...], kvw[...])
    lane = lax.broadcasted_iota(jnp.int32, (VP, LANES), 1)
    table = jnp.zeros((VP, LANES), f32)
    for h in range(HEADS):
        at = h // 2 * LANES
        prod = w[:, at : at + LANES] * query[:, at : at + LANES]
        total = jnp.sum(half_of(prod, h % 2), axis=1, keepdims=True) * SCORE_SCALE
        table = jnp.where(lane == h, total, table)
    u[...] = table
    count = planes.shape[2]
    for b in range(planes.shape[0]):
        for p in range(PIX):
            pix[p, b * count : (b + 1) * count, :] = planes[b, p].astype(f32)
        mask[b * count : (b + 1) * count, :] = planes[b, PIX, :, :LANES].astype(f32)
    live = mask[:, :1] > 0.0
    rows = pix.shape[2]
    for pair in range(HEADS // 2):
        pieces = []
        at = pair * LANES
        for half in range(2):
            h = pair * 2 + half
            scores = jnp.zeros((VARS, rows), f32)
            for p in range(PIX):
                scores += pix[p] * u[p * VARS : (p + 1) * VARS, h : h + 1]
            scores = jnp.where(live, scores, NEG_BIG)
            highest = jnp.max(scores, axis=0, keepdims=True)
            exponent = jnp.where(live, jnp.exp(scores - highest), 0.0)
            prob = exponent / jnp.sum(exponent, axis=0, keepdims=True)
            probs[h] = prob
            weighted = jnp.concatenate([pix[p] * prob for p in range(PIX)], axis=0)
            pieces.append(nn_f32(weighted, w[:, D + at : D + at + LANES], ((0,), (0,))))
        both = jnp.where(lane_half(pieces[0].shape), pieces[0], pieces[1])
        agg_low[:, at : at + LANES] = both.astype(bf16)
    residual = nn(agg_low[...], aggw[...])
    res[...] = residual
    normed, unused = norm_stats(residual)
    hid[...] = (normed * (1.0 + mod_row(mod, 1)) + mod_row(mod, 0)).astype(bf16)


def agg_bwd_kernel(
    go, agg_low, probs, w, u, e, kvw, aggw, query, pix,
    planes, sec,
    sec32, gv, gk, pixg,
):
    rows = pix.shape[2]
    grad_res = go[...].astype(bf16)
    agg_grad = tn(agg_low[...], grad_res)
    start = EMBED_LINES + DB + KV_LINES
    for c in range(DB):
        sec32[pl.ds(start + c, D, stride=DB), :] = agg_grad[:, c * LANES : (c + 1) * LANES]
    grad_agg = nt(grad_res, aggw[...]).astype(bf16)
    first = lane_half((VP, LANES))
    pixel_sum = [jnp.zeros((VARS, rows), f32) for p in range(PIX)]
    for p in range(PIX):
        pixg[p] = pixel_sum[p]
    for pair in range(HEADS // 2):
        at = pair * LANES
        ga_pair = grad_agg[:, at : at + LANES]
        w_pair = w[:, D + at : D + at + LANES]
        value_parts = []
        key_parts = []
        for half in range(2):
            h = pair * 2 + half
            prob = probs[h]
            ga_half = half_of(ga_pair, half)
            back = nn_f32(w_pair, ga_half.astype(f32), ((1,), (1,)))
            grad_probs = jnp.zeros((VARS, rows), f32)
            for p in range(PIX):
                grad_probs += pix[p] * back[p * VARS : (p + 1) * VARS, :]
            inner = jnp.sum(prob * grad_probs, axis=0, keepdims=True)
            grad_scores = prob * (grad_probs - inner)
            sums = []
            for p in range(PIX):
                here = slice(p * VARS, (p + 1) * VARS)
                pixg[p] += grad_scores * u[here, h : h + 1] + prob * back[here, :]
                sums.append(jnp.sum(pix[p] * grad_scores, axis=1, keepdims=True))
            key_parts.append(jnp.concatenate(sums, axis=0) * SCORE_SCALE)
            weighted = jnp.concatenate([pix[p] * prob for p in range(PIX)], axis=0)
            value_parts.append(nn(weighted.astype(bf16), ga_half))
        gv[:, at : at + LANES] = jnp.where(first, value_parts[0], value_parts[1])
        gk[:, at : at + LANES] = jnp.where(first, key_parts[0], key_parts[1])
    count = planes.shape[2]
    for b in range(planes.shape[0]):
        for p in range(PIX):
            planes[b, p] = pixg[p, b * count : (b + 1) * count, :]
    query_grad = jnp.sum(gk[...] * w[:, :D], axis=0, keepdims=True)
    for c in range(DB):
        sec32[EMBED_LINES + c : EMBED_LINES + c + 1, :] = query_grad[:, c * LANES : (c + 1) * LANES]
    grad_kv = jnp.concatenate([gk[...] * query[...], gv[...]], axis=1).astype(bf16)
    kv_grad = tn(e[...], grad_kv)
    start = EMBED_LINES + DB
    for c in range(2 * DB):
        sec32[pl.ds(start + c, D, stride=2 * DB), :] = kv_grad[:, c * LANES : (c + 1) * LANES]
    embed_grad = nt(grad_kv, kvw[...])
    for p in range(PIX):
        for c in range(DB):
            sec32[pl.ds(p * DB + c, VARS, stride=PIX * DB), :] = embed_grad[
                p * VARS : (p + 1) * VARS, c * LANES : (c + 1) * LANES
            ]
    tail = up16(HEAD_LINES) - HEAD_LINES
    sec32[HEAD_LINES:, :] = jnp.zeros((tail, LANES), f32)
    narrow_lines(sec32, up16(HEAD_LINES), sec)


def unpack_kernel(source, base, start, *refs):
    pieces = refs[: len(source.arrays)]
    qkvw, projw, upw, downw, lines = refs[len(source.arrays) :]
    source.load(pieces, base, lines)
    start = start - base
    unpack(lines, start, D, 3 * DB, qkvw)
    start += QKV_LINES
    unpack(lines, start, D, DB, projw)
    start += PROJ_LINES
    unpack(lines, start, D, FF // LANES, upw)
    start += FF_LINES
    unpack(lines, start, FF, DB, downw)


def gelu_parts(value):
    scale = math.sqrt(2.0 / math.pi)
    square = value * value
    tanh = jnp.tanh(scale * (value + 0.044715 * value * square))
    half = 0.5 * (1.0 + tanh)
    slope = half + 0.5 * value * (1.0 - tanh * tanh) * scale * (1.0 + 3.0 * 0.044715 * square)
    return value * half, slope


def pair_columns(pair):
    return [pl.ds(pl.multiple_of(pair * LANES + i * D, LANES), LANES) for i in range(3)]


def key_bias(rels, limits, rows):
    parts = []
    for rel in rels:
        position = (limits[1] ^ rel) * rows + lax.broadcasted_iota(jnp.int32, (1, rows), 1)
        parts.append(jnp.where(position < limits[0], 0.0, NEG_BIG))
    return jnp.concatenate(parts, axis=1)


def near_attend_kernel(rels, limits, *refs):
    hidden = refs[: len(rels)]
    qkvw, qkv, acc, peak, total = refs[len(rels) :]
    rows = acc.shape[0]
    for i in range(len(rels)):
        qkv[i * rows : (i + 1) * rows, :] = nn(hidden[i][...], qkvw[...]).astype(bf16)
    bias = key_bias(rels, limits, rows)
    first = lane_half((rows, LANES))
    lane = lax.broadcasted_iota(jnp.int32, (rows, LANES), 1)
    peak[...] = jnp.zeros((rows, LANES), f32)
    total[...] = jnp.zeros((rows, LANES), f32)

    def attend(pair, carry):
        at, k_at, v_at = pair_columns(pair)
        query = qkv[:rows, at] * SCORE_SCALE
        parts = []
        for half in range(2):
            scores = nt(half_of(query, half), qkv[:, k_at]) + bias
            highest = jnp.max(scores, axis=1, keepdims=True)
            exponent = jnp.exp(scores - highest)
            parts.append(nn(exponent.astype(bf16), qkv[:, v_at]))
            here = lane == pair * 2 + half
            peak[...] = jnp.where(here, highest, peak[...])
            total[...] = jnp.where(here, jnp.sum(exponent, axis=1, keepdims=True), total[...])
        acc[:, at] = jnp.where(first, parts[0], parts[1])
        return carry

    lax.fori_loop(0, HEADS // 2, attend, 0)


def layer_fwd_kernel(near, far, limits, *refs):
    hidden = refs[: len(far)]
    (qkv_near, acc, peak, near_total, res, mod, mod_next, qkvw, projw, upw, downw) = refs[
        len(far) : len(far) + 11
    ]
    (qkv, att, lse, b1, mid, pre, b2, res_next, hid_next, h_low, a_low, qkv_far) = refs[
        len(far) + 11 :
    ]
    mine = limits[1]
    rows = res.shape[0]
    for i, rel in enumerate(near):
        at = pl.multiple_of((mine ^ rel) * rows, rows)
        qkv[pl.ds(at, rows), :] = qkv_near[i * rows : (i + 1) * rows, :]
    for i, rel in enumerate(far):
        at = pl.multiple_of((mine ^ rel) * rows, rows)
        block = nn(hidden[i][...], qkvw[...]).astype(bf16)
        qkv_far[i * rows : (i + 1) * rows, :] = block
        qkv[pl.ds(at, rows), :] = block
    bias = key_bias(far, limits, rows)
    first = lane_half((rows, LANES))
    lane = lax.broadcasted_iota(jnp.int32, (rows, LANES), 1)
    lse[...] = jnp.zeros((rows, LANES), f32)

    def attend(pair, carry):
        at, k_at, v_at = pair_columns(pair)
        query = qkv_near[:rows, at] * SCORE_SCALE
        parts = []
        for half in range(2):
            here = lane == pair * 2 + half
            before = jnp.sum(jnp.where(here, peak[...], 0.0), axis=1, keepdims=True)
            total = jnp.sum(jnp.where(here, near_total[...], 0.0), axis=1, keepdims=True)
            scores = nt(half_of(query, half), qkv_far[:, k_at]) + bias
            highest = jnp.maximum(before, jnp.max(scores, axis=1, keepdims=True))
            exponent = jnp.exp(scores - highest)
            factor = jnp.exp(before - highest)
            total = total * factor + jnp.sum(exponent, axis=1, keepdims=True)
            weighted = acc[:, at] * factor + nn(exponent.astype(bf16), qkv_far[:, v_at])
            parts.append(weighted * (1.0 / total))
            lse[...] = jnp.where(here, highest + jnp.log(total), lse[...])
        att[:, at] = jnp.where(first, parts[0], parts[1])
        return carry

    lax.fori_loop(0, HEADS // 2, attend, 0)
    branch_one = nn(att[...].astype(bf16), projw[...])
    b1[...] = branch_one
    middle = res[...] + mod_row(mod, 2) * branch_one
    mid[...] = middle
    normed, unused = norm_stats(middle)
    h_low[...] = (normed * (1.0 + mod_row(mod, 4)) + mod_row(mod, 3)).astype(bf16)
    pre[...] = nn(h_low[...], upw[...])
    a_low[...] = gelu_parts(pre[...])[0].astype(bf16)
    branch_two = nn(a_low[...], downw[...])
    b2[...] = branch_two
    result = mid[...] + mod_row(mod, 5) * branch_two
    res_next[...] = result
    normed, unused = norm_stats(result)
    hid_next[...] = (normed * (1.0 + mod_row(mod_next, 1)) + mod_row(mod_next, 0)).astype(bf16)


def mlp_bwd_kernel(
    go, mod, pre, mid, b1, b2, att, lse, upw, downw, projw,
    gmid, ga_ext, delta, sums, act_low, gb2_low, h2_low, gp_low, gb1_low,
):
    rows = go.shape[0]
    grad_out = go[...]
    sums[...] = jnp.zeros(sums.shape, f32)
    put_row(sums, 5, jnp.sum(grad_out * b2[...], axis=0, keepdims=True))
    gb2_low[...] = (mod_row(mod, 5) * grad_out).astype(bf16)
    grad_act = nt(gb2_low[...], downw[...])
    act, slope = gelu_parts(pre[...])
    act_low[...] = act.astype(bf16)
    gp_low[...] = (grad_act * slope).astype(bf16)
    grad_hidden = nt(gp_low[...], upw[...])
    normed, inverse = norm_stats(mid[...])
    scale = 1.0 + mod_row(mod, 4)
    h2_low[...] = (normed * scale + mod_row(mod, 3)).astype(bf16)
    put_row(sums, 3, jnp.sum(grad_hidden, axis=0, keepdims=True))
    put_row(sums, 4, jnp.sum(grad_hidden * normed, axis=0, keepdims=True))
    grad_mid = grad_out + norm_back(grad_hidden * scale, normed, inverse)
    gmid[...] = grad_mid
    put_row(sums, 2, jnp.sum(grad_mid * b1[...], axis=0, keepdims=True))
    gb1_low[...] = (mod_row(mod, 2) * grad_mid).astype(bf16)
    grad_att = nt(gb1_low[...], projw[...]).astype(bf16)
    ga_ext[:rows, :] = grad_att
    lane = lax.broadcasted_iota(jnp.int32, (rows, LANES), 1)
    table = jnp.zeros((rows, LANES), f32)
    for h in range(HEADS):
        at = h // 2 * LANES
        prod = grad_att[:, at : at + LANES].astype(f32) * att[:, at : at + LANES]
        total = jnp.sum(half_of(prod, h % 2), axis=1, keepdims=True)
        table = jnp.where(lane == h, total, table)
    delta[...] = table
    both = jnp.where(lane < 8, lse[...], pltpu.roll(table, 8, 1))
    stats = jnp.transpose(both)[:16, :]
    high = stats.astype(bf16)
    low = (stats - high.astype(f32)).astype(bf16)
    ga_ext[rows:, :] = jnp.zeros((32, D), bf16)
    ga_ext[rows : rows + 16, :rows] = high
    ga_ext[rows + 16 : rows + 32, :rows] = low


def mlp_grads_kernel(shift, act_low, gb2_low, h2_low, gp_low, att, gb1_low, sec, sec32):
    lead = jnp.zeros((16, LANES), f32)
    sec32[0:16, :] = lead
    sec32[sec32.shape[0] - 16 :, :] = lead
    start = shift
    proj = tn(att[...].astype(bf16), gb1_low[...])
    for c in range(DB):
        sec32[pl.ds(start + c, D, stride=DB), :] = proj[:, c * LANES : (c + 1) * LANES]
    start += PROJ_LINES
    width = FF // LANES
    for c in range(0, width, 2):
        part = tn(h2_low[...], gp_low[:, c * LANES : (c + 2) * LANES])
        for k in range(2):
            sec32[pl.ds(start + c + k, D, stride=width), :] = part[
                :, k * LANES : (k + 1) * LANES
            ]
    start += FF_LINES
    for r in range(0, FF, D):
        part = tn(act_low[:, r : r + D], gb2_low[...])
        for c in range(DB):
            sec32[pl.ds(start + r * DB + c, D, stride=DB), :] = part[
                :, c * LANES : (c + 1) * LANES
            ]
    narrow_lines(sec32, sec32.shape[0], sec)


def query_bwd_kernel(limits, qkv, ga_ext, lse, delta, gq):
    length = limits[0]
    mine = limits[1]
    rows = lse.shape[0]
    seq_len = qkv.shape[0]
    position = lax.broadcasted_iota(jnp.int32, (1, seq_len), 1)
    bias = jnp.where(position < length, 0.0, NEG_BIG)
    own = pl.ds(pl.multiple_of(mine * rows, rows), rows)
    first = lane_half((rows, LANES))
    lane = lax.broadcasted_iota(jnp.int32, (rows, LANES), 1)

    def column(ref, index):
        return jnp.sum(jnp.where(lane == index, ref[...], 0.0), axis=1, keepdims=True)

    def one_pair(pair, carry):
        at, k_at, v_at = (pl.ds(pl.multiple_of(pair * LANES + i * D, LANES), LANES) for i in range(3))
        query = qkv[own, at] * SCORE_SCALE
        keys = qkv[:, k_at]
        values = qkv[:, v_at]
        grad_pair = ga_ext[:rows, at]
        parts = []
        for half in range(2):
            h = pair * 2 + half
            scores = nt(half_of(query, half), keys) + bias
            prob = jnp.exp(scores - column(lse, h))
            grad_prob = nt(half_of(grad_pair, half), values)
            grad_score = (prob * (grad_prob - column(delta, h))).astype(bf16)
            parts.append(nn(grad_score, keys) * SCORE_SCALE)
        gq[:, at] = jnp.where(first, parts[0], parts[1]).astype(bf16)
        return carry

    lax.fori_loop(0, HEADS // 2, one_pair, 0)


def keys_sums(rels, pieces, limits, qkv, stats, rows, store):
    mine = limits[1]
    own = pl.ds(pl.multiple_of(mine * rows, rows), rows)
    first = lane_half((rows, LANES))
    for i in range(len(rels)):
        both = pieces[i][rows : rows + 32, :rows].astype(f32)
        stats[i] = both[:16, :] + both[16:, :]

    def one_pair(pair, carry):
        at, k_at, v_at = (pl.ds(pl.multiple_of(pair * LANES + i * D, LANES), LANES) for i in range(3))
        keys = qkv[own, k_at] * SCORE_SCALE
        values = qkv[own, v_at]
        key_parts = []
        value_parts = []
        for half in range(2):
            h = pair * 2 + half
            key_half = half_of(keys, half)
            value_half = half_of(values, half)
            key_sum = jnp.zeros((rows, LANES), f32)
            value_sum = jnp.zeros((rows, LANES), f32)
            for i, rel in enumerate(rels):
                there = pl.ds(pl.multiple_of((mine ^ rel) * rows, rows), rows)
                query = qkv[there, at]
                grad_pair = pieces[i][:rows, at]
                prob = jnp.exp(nt(key_half, query) - stats[i, pl.ds(h, 1), :])
                grad_prob = nt(value_half, grad_pair)
                grad_score = (prob * (grad_prob - stats[i, pl.ds(8 + h, 1), :])).astype(bf16)
                key_sum += nn(grad_score, query)
                value_sum += nn(prob.astype(bf16), grad_pair)
            key_parts.append(key_sum * SCORE_SCALE)
            value_parts.append(value_sum)
        store(
            at,
            jnp.where(first, key_parts[0], key_parts[1]),
            jnp.where(first, value_parts[0], value_parts[1]),
        )
        return carry

    lax.fori_loop(0, HEADS // 2, one_pair, 0)


def near_keys_kernel(rels, limits, *refs):
    pieces = refs[: len(rels)]
    qkv, key_out, value_out, stats = refs[len(rels) :]

    def store(at, key_sum, value_sum):
        key_out[:, at] = key_sum
        value_out[:, at] = value_sum

    keys_sums(rels, pieces, limits, qkv, stats, key_out.shape[0], store)


def keys_bwd_kernel(rels, limits, *refs):
    pieces = refs[: len(rels)]
    (qkv, gq, key_near, value_near, res, mod, qkvw, gmid) = refs[len(rels) : len(rels) + 8]
    (gqkv, go_prev, sums, stats) = refs[len(rels) + 8 :]
    rows = res.shape[0]
    position = limits[1] * rows + lax.broadcasted_iota(jnp.int32, (rows, 1), 0)
    live = position < limits[0]
    gqkv[:, :D] = gq[...]

    def store(at, key_sum, value_sum):
        k_at, v_at = (pl.ds(pl.multiple_of(at.start + i * D, LANES), LANES) for i in (1, 2))
        gqkv[:, k_at] = jnp.where(live, key_near[:, at] + key_sum, 0.0).astype(bf16)
        gqkv[:, v_at] = jnp.where(live, value_near[:, at] + value_sum, 0.0).astype(bf16)

    keys_sums(rels, pieces, limits, qkv, stats, rows, store)
    grad_hidden = nt(gqkv[...], qkvw[...])
    normed, inverse = norm_stats(res[...])
    sums[...] = jnp.zeros(sums.shape, f32)
    put_row(sums, 0, jnp.sum(grad_hidden, axis=0, keepdims=True))
    put_row(sums, 1, jnp.sum(grad_hidden * normed, axis=0, keepdims=True))
    scale = 1.0 + mod_row(mod, 1)
    go_prev[...] = gmid[...] + norm_back(grad_hidden * scale, normed, inverse)


def qkv_grads_kernel(shift, hidden, gqkv, sec, sec32):
    sec32[0:16, :] = jnp.zeros((16, LANES), f32)
    sec32[sec32.shape[0] - 16 :, :] = jnp.zeros((16, LANES), f32)
    width = 3 * DB
    for c in range(0, width, DB):
        part = tn(hidden[...], gqkv[:, c * LANES : (c + DB) * LANES])
        for k in range(DB):
            sec32[pl.ds(shift + c + k, D, stride=width), :] = part[:, k * LANES : (k + 1) * LANES]
    narrow_lines(sec32, sec32.shape[0], sec)


def axis_dims(axis, count):
    dims = []
    for bit in range((count - 1).bit_length()):
        dims.append((axis, [i ^ (1 << bit) for i in range(count)], [i >> bit & 1 for i in range(count)]))
    return dims


def together(values):
    return lax.optimization_barrier(values)


def total_of(parts, begin, end):
    return sum(part[begin:end].astype(f32) for part in parts)


class Cube:
    def __init__(self, var_count, dp_count):
        self.dp_count = dp_count
        self.owners = var_count * dp_count
        var_dims = axis_dims("var", var_count)
        self.core = var_dims[0]
        self.dims = var_dims[1:] + axis_dims("dp", dp_count)

    def partner(self, owner, dim):
        axis, partner, unused = dim
        v, d = divmod(owner, self.dp_count)
        if axis == "var":
            return partner[v] * self.dp_count + d
        return v * self.dp_count + partner[d]

    def bit(self, owner, dim):
        axis, unused, bits = dim
        v, d = divmod(owner, self.dp_count)
        return bits[v] if axis == "var" else bits[d]

    def hop(self, value, *dims, core=None):
        pairs = []
        for owner in range(self.owners):
            other = owner
            for dim in dims:
                other = self.partner(other, dim)
            if core is None or self.bit(owner, self.core) == core:
                pairs.append((owner, other))
        return self.send(value, pairs)

    def send(self, value, pairs):
        return lax.ppermute(value, ("var", "dp"), pairs)

    def mine(self):
        return lax.axis_index("var") * self.dp_count + lax.axis_index("dp")

    def exchange_sum(self, value, groups):
        for group in groups:
            terms = [value]
            for mask in range(1, 2 ** len(group)):
                terms.append(self.hop(value, *[d for i, d in enumerate(group) if mask >> i & 1]))
            while len(terms) > 1:
                terms = [terms[i] + terms[i + 1] for i in range(0, len(terms), 2)]
            value = terms[0]
        return value


PLAN_SHAPE = (4, 8, 1440)
HALF = 720
NEEDED_ZERO = {0: 3, 1: 3, 2: 3, 3: 1, 7: 2, 16: 3, 17: 3, 22: 3, 23: 3}
ENTRIES = (
    [(o, h) for o in (0, 1, 2) for h in (0, 1)]
    + [(3, 0), (7, 1)]
    + [(o, h) for o in range(8, 18) for h in (0, 1)]
    + [(o, h) for o in range(22, 32) for h in (0, 1)]
)


class Plan:
    def __init__(self, cube):
        self.cube = cube
        x, y, step, pair = cube.dims
        self.pair = pair
        self.orders = ((y, x, step), (step, y, x), (step, x, y))
        self.back_orders = ((y, x, step), (x, step, y), (step, y, x))
        back = [order[::-1] for order in self.back_orders]
        rows = [
            self.codes(o, self.orders) + self.codes(o, back) + self.flags(o)
            for o in range(cube.owners)
        ]
        row = jnp.asarray(rows, jnp.int32)[cube.mine()]
        self.table = row[: len(ENTRIES)]
        self.back_table = row[len(ENTRIES) : 2 * len(ENTRIES)]
        self.flag = [row[2 * len(ENTRIES) + i] == 1 for i in range(3)]
        ones = [o for o in range(cube.owners) if cube.bit(o, cube.core)]
        self.ones_pairs = [(o, cube.partner(o, pair)) for o in ones]
        self.zero_pairs = [(o, cube.partner(o, pair)) for o in NEEDED_ZERO]

    def flags(self, device):
        needed = NEEDED_ZERO.get(device, 0)
        return [self.cube.bit(device, self.cube.core), needed & 1, needed >> 1]

    def codes(self, device, orders):
        cube = self.cube
        codes = []
        for owner, half in ENTRIES:
            chunk = 1 + half
            stream = cube.bit(owner, cube.core)
            if stream == 1 and cube.bit(owner, self.pair) == cube.bit(device, self.pair):
                chunk = 0
                stream = 1 - half
            place = 0
            for s, dim in enumerate(orders[chunk]):
                place += (cube.bit(owner, dim) ^ cube.bit(device, dim)) << s
            codes.append(chunk * 16 + (stream ^ cube.bit(device, cube.core)) * 8 + place)
        return codes

    def gather(self, shard, sums, first_work, planes, second_work):
        cube = self.cube
        is_one, own_first, own_second = self.flag

        def hop(chunk, step):
            return cube.hop(current[chunk], self.orders[chunk][step])

        def grow(chunk, got):
            current[chunk] = jnp.concatenate([current[chunk], got], axis=0)

        lower = cube.hop(shard[HALF:], cube.core)
        from_one = cube.send(shard, self.ones_pairs)
        from_zero = cube.send(shard, self.zero_pairs)
        current = [jnp.where(is_one, shard[:HALF], lower)[None], None, None]
        grow(0, hop(0, 0))
        from_one, from_zero, current[0], sums = together((from_one, from_zero, current[0], sums))
        first = jnp.where(own_first, shard[:HALF], from_zero[:HALF])
        second = jnp.where(own_second, shard[HALF:], from_zero[HALF:])
        current[1] = jnp.where(is_one, from_one[:HALF], first)[None]
        current[2] = jnp.where(is_one, from_one[HALF:], second)[None]
        sums = first_work(sums)
        got = [hop(0, 1), hop(1, 0), hop(2, 0)]
        for chunk in range(3):
            grow(chunk, got[chunk])
        current, sums, planes = together((current, sums, planes))
        done = second_work(planes, sums)
        last = [hop(0, 2), None, None]
        got = [hop(1, 1), hop(2, 1)]
        for chunk in range(2):
            grow(chunk + 1, got[chunk])
        current[1], current[2], done = together((current[1], current[2], done))
        last[1], last[2] = hop(1, 2), hop(2, 2)
        other = [cube.hop(value, cube.core) for value in current]
        other_last = [cube.hop(value, cube.core) for value in last]
        pieces = [entry for group in zip(current, last, other, other_last) for entry in group]
        return pieces, done

    def scatter(self, keep, send, late, work):
        cube = self.cube
        is_one, own_first, own_second = self.flag
        parts = [[a, cube.hop(b, cube.core)] for a, b in zip(keep, send)]
        half = 4
        for step in range(3):
            outs = [total_of(part, half, 2 * half).astype(bf16) for part in parts]
            for q in range(3):
                got = cube.hop(outs[q], self.back_orders[q][step])
                parts[q] = [part[:half] for part in parts[q]] + [got]
            half //= 2
        first, second, third = (total_of(part, 0, 1)[0] for part in parts)
        back = [(b, a) for a, b in self.ones_pairs + self.zero_pairs]
        low = [second.astype(bf16), third.astype(bf16), first.astype(bf16)]
        low[1], low[2] = together((low[1], low[2]))
        partner = [cube.send(part, back).astype(f32) for part in low[:2]]
        lower, late = together((cube.hop(low[2], cube.core), late))
        lower = lower.astype(f32)
        partner[1], late = together((partner[1], work(late)))
        halves = [
            jnp.where(is_one, first, second) + partner[0],
            jnp.where(is_one, lower, third) + partner[1],
        ]
        return jnp.concatenate(halves, axis=0), late


def flip(value, axis, bit):
    count = lax.axis_size(axis)
    return lax.ppermute(value, axis, [(i, i ^ bit) for i in range(count)])


NEAR = (0, 1)


def gather_blocks(value, work):
    count = lax.axis_size("var")
    pieces = {0: value, 1: flip(value, "var", 1)}
    done = work([pieces[r] for r in NEAR])
    bit = count // 2
    while bit > 1:
        got = {r ^ bit: flip(piece, "var", bit) for r, piece in pieces.items() if r % 2 == 0}
        if bit == 2:
            got, done = together((got, done))
        pieces.update(got)
        bit //= 2
    for r in range(2, count, 2):
        pieces[r + 1] = flip(pieces[r], "var", 1)
    return [pieces[r] for r in range(count)], done


def local(pixels, var_mask, lengths, condition, cotangent, master, moment_one, moment_two):
    var_count = lax.axis_size("var")
    dp_count = lax.axis_size("dp")
    var_index = lax.axis_index("var")
    rows = cotangent.shape[1]
    seq_len = rows * var_count
    local_vars = pixels.shape[0]
    shard_lines = master.shape[0] // LANES
    total_lines = shard_lines * var_count * dp_count

    shard = master.astype(bf16).reshape(shard_lines, LANES)
    present = jnp.where(var_mask == 1, 1.0, 0.0).astype(bf16)
    planes = jnp.concatenate(
        [pixels[:, :, 0, :], jnp.broadcast_to(present[:, None, None], (local_vars, 1, seq_len))],
        axis=1,
    )
    planes = planes.reshape(local_vars, PIX + 1, var_count, rows).transpose(2, 1, 0, 3)

    def spread(values):
        return lax.all_to_all(values, "var", 0, 0, tiled=True)

    cube = Cube(var_count, dp_count)
    planned = (var_count, dp_count, shard_lines) == PLAN_SHAPE
    cond_low = jax.nn.silu(condition.astype(f32)).astype(bf16)
    limits = jnp.stack([lengths[0], var_index.astype(jnp.int32)])
    if planned:
        plan = Plan(cube)
        dp_index = lax.axis_index("dp")
        slots = LAYERS * BIAS_LINES
        x = cube.dims[0]

        def to_all(value):
            copies = jnp.broadcast_to(value[None], (dp_count,) + value.shape)
            return lax.all_to_all(copies, "dp", 0, 0, tiled=True)

        conds = to_all(cond_low[0].reshape(DB, LANES)).reshape(dp_count, D)
        of_slot = jnp.arange(dp_count * slots) // slots
        ada_table, partial = run(
            functools.partial(ada_kernel, shard_lines),
            "ada",
            [shape((shard_lines, dp_count * slots), bf16), shape((dp_count * slots, LANES), f32)],
            [
                cube.mine()[None].astype(jnp.int32), shard, conds,
                (jnp.arange(dp_count)[:, None] == of_slot[None, :]).astype(bf16),
                (jnp.arange(dp_count * slots) % slots)[None, :].astype(jnp.int32),
            ],
            [SM] + [VM] * 4,
            [pltpu.VMEM((shard_lines, D), bf16)],
            flops=10**9,
        )
        def first_work(sums):
            sums = sums.reshape(dp_count, slots, LANES)
            return jnp.sum(lax.all_to_all(sums, "dp", 0, 0, tiled=True), axis=0)

        def second_work(these, sums):
            return spread(these), cube.exchange_sum(sums, [[cube.core], [x]])

        pieces, (planes, own) = plan.gather(shard, partial, first_work, planes, second_work)
        arrays = [plan.table, *pieces]
        specs = [SM] + [VM] * len(pieces)
        mods = [own[layer * BIAS_LINES : (layer + 1) * BIAS_LINES] for layer in range(LAYERS)]
    else:
        planes = spread(planes)
        arrays = [lax.all_gather(shard, ("var", "dp"), axis=0, tiled=True)]
        specs = [VM]
        mods = []
        for layer in range(LAYERS):
            start = HEAD_LINES + layer * LAYER_LINES
            ada = arrays[0][start : start + ADA_LINES].reshape(D, 6 * D)
            bias = arrays[0][start + ADA_LINES : start + ADA_LINES + BIAS_LINES]
            mods.append(
                jnp.dot(cond_low, ada, preferred_element_type=f32).reshape(BIAS_LINES, LANES)
                + bias.astype(f32)
            )
    mods = [jnp.pad(mod, ((0, 24 - BIAS_LINES), (0, 0))) for mod in mods]
    source = Source(arrays, specs, planned)

    begin, end = source.span(0, HEAD_LINES)
    (residual, hidden, agg_low, probs, w, u, e, kvw, aggw, query, pix) = run(
        functools.partial(agg_fwd_kernel, source),
        "agg_fwd",
        [
            shape((rows, D), f32), shape((rows, D), bf16), shape((rows, D), bf16),
            shape((HEADS, VARS, rows), f32), shape((VP, 2 * D), f32), shape((VP, LANES), f32),
            shape((VP, D), bf16), shape((D, 2 * D), bf16), shape((D, D), bf16),
            shape((1, D), f32), shape((PIX, VARS, rows), f32),
        ],
        [*arrays, planes, mods[0]],
        [*specs, VM, VM],
        [
            pltpu.VMEM((end - begin, LANES), f32), pltpu.VMEM((VP, D), f32),
            pltpu.VMEM((VARS, LANES), f32),
        ],
        flops=10**9,
    )

    def unpack_layer(layer):
        start = HEAD_LINES + layer * LAYER_LINES + ADA_LINES + BIAS_LINES
        begin, end = source.span(start, HEAD_LINES + (layer + 1) * LAYER_LINES)
        return run(
            functools.partial(unpack_kernel, source, begin, start),
            f"unpack_{layer}",
            [
                shape((D, 3 * D), bf16), shape((D, D), bf16), shape((D, FF), bf16),
                shape((FF, D), bf16),
            ],
            arrays,
            specs,
            [pltpu.VMEM((end - begin, LANES), f32)],
            flops=10**9,
        )

    weights = [None] * LAYERS

    def begin_layer(layer, value):
        def work(blocks):
            weights = unpack_layer(layer)
            return weights, run(
                functools.partial(near_attend_kernel, NEAR),
                f"near_attend_{layer}",
                [
                    shape((len(NEAR) * rows, 3 * D), bf16), shape((rows, D), f32),
                    shape((rows, LANES), f32), shape((rows, LANES), f32),
                ],
                [limits, *blocks, weights[0]],
                [SM] + [VM] * (len(NEAR) + 1),
                flops=10**9,
            )

        blocks, (weights[layer], attention) = gather_blocks(value, work)
        return blocks, attention

    hidden_blocks, partial_attention = begin_layer(0, hidden)

    stored = []
    for layer in range(LAYERS):
        qkvw, projw, upw, downw = weights[layer]
        mod = mods[layer]
        mod_next = mods[min(layer + 1, LAYERS - 1)]
        blocks = hidden_blocks
        outs = [
            shape((seq_len, 3 * D), bf16), shape((rows, D), f32), shape((rows, LANES), f32),
            shape((rows, D), f32), shape((rows, D), f32), shape((rows, FF), f32),
            shape((rows, D), f32), shape((rows, D), f32), shape((rows, D), bf16),
        ]
        near, far = NEAR, tuple(range(len(NEAR), var_count))
        qkv, att, lse, b1, mid, pre, b2, next_residual, next_hidden = run(
            functools.partial(layer_fwd_kernel, near, far),
            f"layer_fwd_{layer}",
            outs,
            [
                limits, *(blocks[r] for r in far), *partial_attention, residual, mod, mod_next,
                qkvw, projw, upw, downw,
            ],
            [SM] + [VM] * (len(far) + 11),
            [
                pltpu.VMEM((rows, D), bf16), pltpu.VMEM((rows, FF), bf16),
                pltpu.VMEM((len(far) * rows, 3 * D), bf16),
            ],
            flops=4 * 10**9,
        )
        stored.append((hidden, residual, qkv, att, lse, b1, mid, pre, b2))
        residual, hidden = next_residual, next_hidden
        if layer + 1 < LAYERS:
            hidden_blocks, partial_attention = begin_layer(layer + 1, hidden)
    output = residual

    grad_out = cotangent[0]
    sections = []
    ada_sums = [None] * LAYERS
    for layer in reversed(range(LAYERS)):
        qkvw, projw, upw, downw = weights[layer]
        mod = mods[layer]
        hidden, residual, qkv, att, lse, b1, mid, pre, b2 = stored[layer]
        first_line = HEAD_LINES + layer * LAYER_LINES
        outs = [
            shape((rows, D), f32), shape((rows + 32, D), bf16), shape((rows, LANES), f32),
            shape((24, LANES), f32), shape((rows, FF), bf16), shape((rows, D), bf16),
            shape((rows, D), bf16), shape((rows, FF), bf16), shape((rows, D), bf16),
        ]
        gmid, ga_ext, delta, sums_a, act_low, gb2_low, h2_low, gp_low, gb1_low = run(
            mlp_bwd_kernel,
            f"mlp_bwd_{layer}",
            outs,
            [grad_out, mod, pre, mid, b1, b2, att, lse, upw, downw, projw],
            flops=2 * 10**9,
        )

        def work(near_blocks, layer=layer, qkv=qkv, ga_ext=ga_ext, lse=lse, delta=delta):
            (gq,) = run(
                query_bwd_kernel,
                f"query_bwd_{layer}",
                [shape((rows, D), bf16)],
                [limits, qkv, ga_ext, lse, delta],
                [SM] + [VM] * 4,
                flops=4 * 10**9,
            )
            return gq, run(
                functools.partial(near_keys_kernel, NEAR),
                f"near_keys_{layer}",
                [shape((rows, D), f32), shape((rows, D), f32)],
                [limits, *near_blocks, qkv],
                [SM] + [VM] * (len(NEAR) + 1),
                [pltpu.VMEM((len(NEAR), 16, rows), f32)],
                flops=3 * 10**9,
            )

        blocks, (gq, (key_near, value_near)) = gather_blocks(ga_ext, work)
        start = first_line + ADA_LINES + BIAS_LINES + QKV_LINES
        count = up16(start + PROJ_LINES + 2 * FF_LINES) - down16(start)
        (section,) = run(
            functools.partial(mlp_grads_kernel, start - down16(start)),
            f"mlp_grads_{layer}",
            [shape((count, LANES), bf16)],
            [act_low, gb2_low, h2_low, gp_low, att, gb1_low],
            scratch=[pltpu.VMEM((count, LANES), f32)],
            flops=2 * 10**9,
        )
        sections.append((start, PROJ_LINES + 2 * FF_LINES, section))
        far = tuple(range(len(NEAR), var_count))
        gqkv, grad_out, sums_b = run(
            functools.partial(keys_bwd_kernel, far),
            f"keys_bwd_{layer}",
            [shape((rows, 3 * D), bf16), shape((rows, D), f32), shape((24, LANES), f32)],
            [
                limits, *(blocks[r] for r in far), qkv, gq, key_near, value_near, residual, mod, qkvw,
                gmid,
            ],
            [SM] + [VM] * (len(far) + 8),
            [pltpu.VMEM((len(far), 16, rows), f32)],
            flops=3 * 10**9,
        )
        start = first_line + ADA_LINES + BIAS_LINES
        count = up16(start + QKV_LINES) - down16(start)
        (section,) = run(
            functools.partial(qkv_grads_kernel, start - down16(start)),
            f"qkv_grads_{layer}",
            [shape((count, LANES), bf16)],
            [hidden, gqkv],
            scratch=[pltpu.VMEM((count, LANES), f32)],
            flops=10**9,
        )
        sections.append((start, QKV_LINES, section))
        ada_sums[layer] = (sums_a + sums_b)[:BIAS_LINES]

    pixel_grad, section = run(
        agg_bwd_kernel,
        "agg_bwd",
        [
            shape((var_count, PIX, local_vars, rows), f32),
            shape((up16(HEAD_LINES), LANES), bf16),
        ],
        [grad_out, agg_low, probs, w, u, e, kvw, aggw, query, pix],
        scratch=[
            pltpu.VMEM((up16(HEAD_LINES), LANES), f32), pltpu.VMEM((VP, D), f32),
            pltpu.VMEM((VP, D), f32), pltpu.VMEM((PIX, VARS, rows), f32),
        ],
        flops=10**9,
    )
    sections.append((0, HEAD_LINES, section))
    def unspread(values):
        return lax.all_to_all(values, "var", 0, 0, tiled=True)

    if planned:
        sections.sort(key=lambda entry: entry[0])
        meta = [(down16(start), part.shape[0]) for start, count, part in sections]
        own = cube.exchange_sum(jnp.concatenate(ada_sums, axis=0), [[cube.core], [x]])
        parts, own = together(([s[2] for s in sections], own))
        packed = run(
            functools.partial(pack_kernel, meta),
            "pack",
            [shape((8, HALF, LANES), bf16)] * 6,
            [
                plan.back_table,
                *parts,
            ],
            [SM] + [VM] * len(sections),
            [pltpu.VMEM((len(ENTRIES) * HALF, LANES), bf16)],
        )

        def beside_scatter(values):
            own, grads = values
            return to_all(own), unspread(grads)

        grad_lines, (sums, pixel_grad) = plan.scatter(
            packed[::2], packed[1::2], (own, pixel_grad), beside_scatter
        )
        sums = sums.reshape(dp_count * slots, LANES)
        high = sums.astype(bf16)
        low = (sums - high.astype(f32)).astype(bf16)
        ada_lines = nn(ada_table, high) + nn(ada_table, low)
        line = cube.mine() * shard_lines + lax.broadcasted_iota(jnp.int32, (shard_lines, 1), 0)
        for layer in range(LAYERS):
            start = HEAD_LINES + layer * LAYER_LINES
            inside = jnp.logical_and(line >= start, line < start + ADA_LINES + BIAS_LINES)
            grad_lines = jnp.where(inside, ada_lines, grad_lines)
    else:
        pixel_grad = unspread(pixel_grad)
        for layer in range(LAYERS):
            start = HEAD_LINES + layer * LAYER_LINES
            outer = cond_low[0].astype(f32)[:, None, None] * ada_sums[layer][None]
            outer = outer.reshape(ADA_LINES, LANES).astype(bf16)
            shift = start - down16(start)
            outer = jnp.concatenate(
                [jnp.zeros((shift, LANES), bf16), outer, ada_sums[layer].astype(bf16)], axis=0
            )
            sections.append((start, ADA_LINES + BIAS_LINES, outer))
        sections.sort(key=lambda entry: entry[0])
        parts = [
            part[start - down16(start) : start - down16(start) + count]
            for start, count, part in sections
        ]
        used = sections[-1][0] + sections[-1][1]
        parts.append(jnp.zeros((total_lines - used, LANES), bf16))
        whole = jnp.concatenate(parts, axis=0)
        grad_lines = lax.psum_scatter(
            whole, ("var", "dp"), scatter_dimension=0, tiled=True
        ).astype(f32)
    patch_grads = pixel_grad.transpose(2, 1, 0, 3).reshape(local_vars, PIX, seq_len)
    grad_shard = grad_lines.reshape(-1)
    squares = jnp.sum(grad_shard * grad_shard)
    if planned:
        copies = jnp.broadcast_to(squares, (cube.owners, 1, LANES))
        copies = lax.all_to_all(copies, ("var", "dp"), 0, 0, tiled=True)
        squares = jnp.sum(copies, axis=0)[0, 0]
    else:
        squares = lax.psum(squares, ("var", "dp"))
    grad_norm = jnp.sqrt(squares)
    clip_limit = CLIP_COEF * math.sqrt(PARAMS * seq_len * dp_count)
    clipped = grad_shard * (clip_limit / jnp.maximum(grad_norm, clip_limit))
    new_one = BETA_ONE * moment_one + (1.0 - BETA_ONE) * clipped
    new_two = BETA_TWO * moment_two + (1.0 - BETA_TWO) * clipped * clipped
    ratio = (
        new_one / (1.0 - BETA_ONE**STEP) / (jnp.sqrt(new_two / (1.0 - BETA_TWO**STEP)) + ADAM_EPS)
    )
    new_master = master - LEARN_RATE * (ratio + WEIGHT_DECAY * master)
    return (
        output[None],
        patch_grads[:, :, None, :],
        grad_norm,
        new_master,
        new_one,
        new_two,
        new_master.astype(bf16),
    )


def solution(mesh):
    in_specs = (
        P("var", None, "dp", None),
        P("var"),
        P("dp"),
        P("dp", None),
        P("dp", "var", None),
        P(("var", "dp")),
        P(("var", "dp")),
        P(("var", "dp")),
    )
    out_specs = (
        P("dp", "var", None),
        P("var", None, "dp", None),
        P(),
        P(("var", "dp")),
        P(("var", "dp")),
        P(("var", "dp")),
        P(("var", "dp")),
    )
    return jax.shard_map(local, mesh=mesh, in_specs=in_specs, out_specs=out_specs, check_vma=False)
```
